512 devices in a mesh: grp: 16 (over z_lo, y), dev: 32 (over x, z_hi, core).
Axes of the slice: x: 4, y: 8, z: 8 (z_hi: 4, z_lo: 2; z = z_hi * 2 + z_lo), core: 2. Of those that a mesh axis runs over, the one named last changes fastest.
Arguments:
- sketch: bfloat16 [1048576, 256], P(('grp', 'dev')), may hold values from -4 to 4
- marginal_std: float32 [1048576], P(('grp', 'dev')), may hold values from 0.1 to 10
- cov_tiles: bfloat16 [9, 256, 256], replicated, may hold values from 0 to 1
- tile_cols: int32 [4096, 9], P(('grp', 'dev')), may hold values from -1 to 4095, as said below
Outputs:
- basis: float32 [1048576, 256], P(('grp', 'dev'))
- factor: float32 [256, 256], replicated
The draws below stay inside these ranges and needn't reach their ends.
Inputs may be any that keep to these rules, and one draw needn't show every extreme that they name: `tile_cols`: tile t holds one line of 256 cells. The lines lie in depth order, except that the order within each aligned block of 4 tiles is permuted. Entry e of the list of tile t is the tile that holds the line e - 4 lines from the line of t (entry 4 is t itself), or -1 where that line lies beyond the ends of the field.
All inputs are finite; a program needn't handle non-finite values.
Results may differ from the reference program's by a relative error of at most 0.0035.
Values may be sent and summed in bfloat16 or wider, within the bound.
A program may use at most 64 MiB of HBM per device.

```python
import math
import jax
import jax.numpy as jnp
from jax import lax

TILE = 256
K = 256
RT = 8
REACH = 4
LAGS = 9
ROWS_DEV = 2048
TILES = 4096
M = 1048576


def draw_sketch(key, part):
    split_keys = jax.random.split(key, 2)
    column_scale = jnp.exp(jax.random.uniform(split_keys[0], (K,), jnp.float32, math.log(0.05), math.log(0.5)))
    values = jnp.clip(jax.random.normal(split_keys[1], (M, K), jnp.float32), -6.0, 6.0)
    return (values * column_scale[None, :]).astype(jnp.bfloat16)


def draw_marginal_std(key, part):
    first_key, second_key = jax.random.split(key)
    block_count = M // ROWS_DEV
    position = (jnp.arange(M, dtype=jnp.int32) // ROWS_DEV).astype(jnp.float32) / max(block_count - 1, 1)
    rise_factor = math.log(3.0)
    local_spread = math.log(2.0)
    block_noise = jax.random.uniform(first_key, (block_count,), jnp.float32, -0.3, 0.3)
    row_noise = jax.random.uniform(second_key, (M,), jnp.float32, -local_spread, local_spread)
    return jnp.exp(rise_factor * (position - 0.5) + jnp.repeat(block_noise, ROWS_DEV) + row_noise)


def draw_cov_tiles(key, part):
    split_keys = jax.random.split(key, 4)
    dip_angle = jax.random.uniform(split_keys[0], (), jnp.float32, -0.5, 0.5)
    radius_along = jax.random.uniform(split_keys[1], (), jnp.float32, 0.6, 1.0)
    radius_across = jax.random.uniform(split_keys[2], (), jnp.float32, 0.9, 1.0)
    nugget = jax.random.uniform(split_keys[3], (), jnp.float32, 0.1, 0.3)
    lag_ids = jnp.arange(LAGS, dtype=jnp.int32) - REACH
    across = lag_ids.astype(jnp.float32) / (REACH + 1)
    cell_ids = jnp.arange(TILE, dtype=jnp.int32)
    along = (cell_ids[None, :] - cell_ids[:, None]).astype(jnp.float32) / (TILE / 4.0)
    first_axis = along[None, :, :] * jnp.cos(dip_angle) + across[:, None, None] * jnp.sin(dip_angle)
    second_axis = -along[None, :, :] * jnp.sin(dip_angle) + across[:, None, None] * jnp.cos(dip_angle)
    distance = jnp.sqrt((first_axis / radius_along) ** 2 + (second_axis / radius_across) ** 2)
    spherical = jnp.where(distance < 1.0, 1.0 - 1.5 * distance + 0.5 * distance ** 3, 0.0)
    same_cell = (lag_ids[:, None, None] == 0) & (cell_ids[:, None] == cell_ids[None, :])[None, :, :]
    values = (1.0 - nugget) * spherical + nugget * same_cell.astype(jnp.float32)
    return values.astype(jnp.bfloat16)


def draw_tile_cols(key, part):
    block_count = TILES // REACH
    slot_ids = jnp.arange(REACH, dtype=jnp.int32)
    scores = jax.random.randint(key, (block_count, REACH), 0, 4096, dtype=jnp.int32) * REACH + slot_ids[None, :]
    slot_lines = jnp.argsort(scores, axis=1).astype(jnp.int32)
    inverse = jnp.argsort(slot_lines, axis=1).astype(jnp.int32)
    tile_ids = jnp.arange(TILES, dtype=jnp.int32)
    block_start = tile_ids // REACH * REACH
    line_of_tile = block_start + slot_lines.reshape(-1)
    tile_of_line = block_start + inverse.reshape(-1)
    lag_ids = jnp.arange(LAGS, dtype=jnp.int32) - REACH
    target = line_of_tile[:, None] + lag_ids[None, :]
    inside = (target >= 0) & (target < TILES)
    safe_target = jnp.clip(target, 0, TILES - 1).astype(jnp.int32)
    return jnp.where(inside, tile_of_line[safe_target], -1).astype(jnp.int32)


def setup_inputs(seed: int = 0) -> dict:
    key_of = jax.random.split(jax.random.key(seed), 5)
    sketch = draw_sketch(jax.random.fold_in(key_of[4], 71), 0)
    marginal_std = draw_marginal_std(jax.random.fold_in(key_of[4], 71), 0)
    cov_tiles = draw_cov_tiles(jax.random.fold_in(key_of[4], 71), 0)
    tile_cols = draw_tile_cols(jax.random.fold_in(key_of[4], 71), 0)
    return dict(sketch=sketch, marginal_std=marginal_std, cov_tiles=cov_tiles, tile_cols=tile_cols)


def reference(sketch, marginal_std, cov_tiles, tile_cols):
    scaled = (sketch.astype(jnp.float32) * marginal_std[:, None]).astype(jnp.bfloat16)
    scaled_tiles = scaled.reshape(TILES, TILE, K)
    present = tile_cols >= 0
    safe_cols = jnp.where(present, tile_cols, 0).astype(jnp.int32)
    correlation = cov_tiles.astype(jnp.float32)

    def block_product(block_pair):
        block_cols, block_present = block_pair
        gathered = scaled_tiles[block_cols.T].astype(jnp.float32)
        gathered = jnp.where(block_present.T[:, :, None, None], gathered, 0.0)
        return jnp.einsum('eij,etjk->tik', correlation, gathered)
    block_count = TILES // RT
    products = lax.map(block_product, (safe_cols.reshape(block_count, RT, LAGS), present.reshape(block_count, RT, LAGS)))
    latent_field = products.reshape(M, K) * marginal_std[:, None]
    gram_matrix = jnp.dot(latent_field.T, latent_field, precision=lax.Precision.HIGHEST) / M
    lower_factor = jnp.linalg.cholesky(gram_matrix)
    basis = lax.linalg.triangular_solve(lower_factor, latent_field, left_side=False, lower=True, transpose_a=True)
    return (basis, lower_factor.T)
```

```python
import functools

import jax
import jax.numpy as jnp
from jax import lax
from jax.experimental import pallas as pl
from jax.experimental.pallas import tpu as pltpu
from jax.sharding import PartitionSpec as P

MESH = pl.DeviceIdType.MESH
F32, BF16 = jnp.float32, jnp.bfloat16
REACH = 4
LINES = 8
LAGS = 9
PANEL = 32
PIVOT = 4

SIZES = dict(nx=4, ny=8, nzh=4, nzl=2)


def far_first(n):
    return sorted(range(1, n), key=lambda k: -min(k, n - k))


def front_kernel(
    sizes, scale, cols_ref, std_ref, sketch_hbm, cov_hbm, high_hbm, low_hbm, gram_ref,
    sketch_v, cov_v, own, below, above, std_sorted, std_cols, acc, high_v, low_v, gacc,
    packed, from_core, part_y, got_y, sum_y, got_z, sum_z, got_x, fin,
    load_sem, store_sem, halo_send, halo_recv, core_send, core_recv, y_send, y_recv,
    z_send, z_recv, x_send, x_recv, g_send, g_recv, f_send, f_recv,
):
    nx, ny, nzh, nzl = sizes["nx"], sizes["ny"], sizes["nzh"], sizes["nzl"]
    nz = nzh * nzl
    grp, dev = lax.axis_index("grp"), lax.axis_index("dev")
    per_grp = nx * nzh * 2
    total = per_grp * ny * nzl
    me = grp * per_grp + dev
    y, z_lo = lax.rem(grp, ny), lax.div(grp, ny)
    core = lax.rem(dev, 2)
    z_hi, x = lax.rem(lax.div(dev, 2), nzh), lax.div(dev, 2 * nzh)
    z = z_hi * nzl + z_lo

    def place(x_, y_, z_, core_):
        return (lax.rem(z_, nzl) * ny + y_, (x_ * nzh + lax.div(z_, nzl)) * 2 + core_)

    def linear(i):
        return (lax.div(i, per_grp), lax.rem(i, per_grp))

    mate = place(x, y, z, 1 - core)
    outer = jnp.where(core == 0, me - 1, me + 1)
    has_outer = (outer >= 0) & (outer < total)
    has_low, has_high = me > 0, me < total - 1

    load_sketch = pltpu.make_async_copy(sketch_hbm, sketch_v, load_sem.at[0])
    load_cov = pltpu.make_async_copy(cov_hbm, cov_v, load_sem.at[1])
    load_sketch.start()
    load_cov.start()

    barrier = pltpu.get_barrier_semaphore()

    def greet(device):
        pl.semaphore_signal(barrier, inc=1, device_id=device, device_id_type=MESH)

    y_peers = [(k, place(x, lax.rem(y + k, ny), z, core)) for k in far_first(ny)]
    z_peers = [(k, place(x, y, lax.rem(z + k, nz), core)) for k in far_first(nz)]
    x_peers = [(k, place(lax.rem(x + k, nx), y, z, core)) for k in far_first(nx)]
    for _, peer in z_peers + y_peers + x_peers:
        greet(peer)
    greet(mate)

    @pl.when(has_outer)
    def _():
        greet(linear(outer))

    tile_of_line = []
    for block in range(LINES // REACH):
        head = block * REACH
        start = cols_ref[head, REACH]
        offset = jnp.int32(0)
        for e in range(REACH):
            offset += jnp.where(cols_ref[head, e] >= start, 1, 0)
        for j in range(REACH):
            tile = cols_ref[head, REACH - offset + j] - start
            tile_of_line.append(jnp.clip(tile, 0, REACH - 1) + head)

    zero_lines = jnp.zeros((REACH,) + own.shape[1:], BF16)
    own[0:REACH] = zero_lines
    own[REACH + LINES :] = zero_lines

    @pl.when(jnp.logical_not(has_low))
    def _():
        below[...] = zero_lines

    @pl.when(jnp.logical_not(has_high))
    def _():
        above[...] = zero_lines

    for j in range(LINES):
        std_sorted[2 * j : 2 * j + 2, :] = std_ref[tile_of_line[j]]
    std_cols[...] = std_sorted[...].T

    def std_of(j):
        return jnp.concatenate([std_cols[:, 2 * j : 2 * j + 1], std_cols[:, 2 * j + 1 : 2 * j + 2]], axis=0)

    load_sketch.wait()
    for j in (0, 7, 1, 6, 2, 5, 3, 4):
        own[REACH + j] = (sketch_v[tile_of_line[j]].astype(F32) * std_of(j)).astype(BF16)
    gacc[...] = jnp.zeros_like(gacc)

    peers = len(y_peers) + len(z_peers) + len(x_peers) + 1
    pl.semaphore_wait(barrier, peers + jnp.where(has_outer, 1, 0))

    def to_low(q):
        return pltpu.make_async_remote_copy(
            src_ref=own.at[REACH + q], dst_ref=above.at[q], send_sem=halo_send.at[q],
            recv_sem=halo_recv.at[q], device_id=linear(me - 1), device_id_type=MESH,
        )

    def to_high(q):
        return pltpu.make_async_remote_copy(
            src_ref=own.at[REACH + LINES - 1 - q], dst_ref=below.at[q], send_sem=halo_send.at[REACH + q],
            recv_sem=halo_recv.at[REACH + q], device_id=linear(me + 1), device_id_type=MESH,
        )

    @pl.when(has_low)
    def _():
        for q in range(REACH):
            to_low(q).start()

    @pl.when(has_high)
    def _():
        for q in range(REACH):
            to_high(q).start()

    load_cov.wait()

    def own_line(j, carry):
        lags = jnp.concatenate([cov_v[e] for e in range(LAGS)], axis=1)
        lines = own[pl.ds(j, LAGS)].reshape(LAGS * own.shape[1], own.shape[2])
        acc[j] = jnp.dot(lags, lines, preferred_element_type=F32)
        return carry

    lax.fori_loop(0, LINES, own_line, 0)

    def finish(j, product):
        latent = product * std_of(j)
        high = latent.astype(BF16)
        low = (latent - high.astype(F32)).astype(BF16)
        high_v[j] = high
        low_v[j] = low
        pair = jnp.concatenate([high, low], axis=1)
        gacc[...] += lax.dot_general(high, pair, (((0,), (0,)), ((), ())), preferred_element_type=F32)
        pltpu.make_async_copy(high_v.at[j], high_hbm.at[j], store_sem.at[j]).start()
        pltpu.make_async_copy(low_v.at[j], low_hbm.at[j], store_sem.at[LINES + j]).start()

    for q in range(REACH):
        @pl.when(has_low)
        def _():
            to_high(q).wait_recv()

        for j in range(REACH - q):
            e = (-1 - q) - j + REACH
            product = acc[j] + jnp.dot(cov_v[e], below[q], preferred_element_type=F32)
            if j == REACH - 1 - q:
                finish(j, product)
            else:
                acc[j] = product

        @pl.when(has_high)
        def _():
            to_low(q).wait_recv()

        for j in range(REACH + q, LINES):
            e = (LINES + q) - j + REACH
            product = acc[j] + jnp.dot(cov_v[e], above[q], preferred_element_type=F32)
            if j == REACH + q:
                finish(j, product)
            else:
                acc[j] = product

    half = gacc.shape[0] // 2
    for n, (r, c) in enumerate(((0, 0), (0, half), (half, half))):
        hh = gacc[r : r + half, c : c + half]
        hl = gacc[r : r + half, 2 * half + c : 3 * half + c]
        lh = gacc[c : c + half, 2 * half + r : 3 * half + r].T
        packed[16 * n : 16 * n + 16] = ((hh + (hl + lh)) * scale).reshape(16, 8, 128)

    count = packed.shape[0] // 2
    chunk = count // ny
    swap = pltpu.make_async_remote_copy(
        src_ref=packed.at[pl.ds((1 - core) * count, count)], dst_ref=from_core, send_sem=core_send.at[0],
        recv_sem=core_recv.at[0], device_id=mate, device_id_type=MESH,
    )
    swap.start()
    swap.wait()
    part_y[...] = packed[pl.ds(core * count, count)] + from_core[...]

    copies = []
    for k, peer in y_peers:
        copies.append(pltpu.make_async_remote_copy(
            src_ref=part_y.at[pl.ds(lax.rem(y + k, ny) * chunk, chunk)], dst_ref=got_y.at[k],
            send_sem=y_send.at[k], recv_sem=y_recv.at[k], device_id=peer, device_id_type=MESH,
        ))
        copies[-1].start()
    value = part_y[pl.ds(y * chunk, chunk)]
    for k in range(1, ny):
        pltpu.make_async_copy(got_y.at[k], got_y.at[k], y_recv.at[k]).wait()
        value = value + got_y[k]

    def gather_sum(value, here, n, peers_, source, slots, send, recv):
        source[...] = value
        for k, peer in peers_:
            copies.append(pltpu.make_async_remote_copy(
                src_ref=source, dst_ref=slots.at[here], send_sem=send.at[k], recv_sem=recv.at[k],
                device_id=peer, device_id_type=MESH,
            ))
            copies[-1].start()
        slots[pl.ds(here, 1)] = value[None]
        for k in range(1, n):
            pltpu.make_async_copy(source, source, recv.at[k]).wait()
        out = slots[0]
        for i in range(1, n):
            out = out + slots[i]
        return out

    value = gather_sum(value, z, nz, z_peers, sum_y, got_z, z_send, z_recv)
    value = gather_sum(value, x, nx, x_peers, sum_z, got_x, x_send, x_recv)

    def chunk_of(y_):
        return fin.at[pl.ds(core * count + y_ * chunk, chunk)]

    def pass_on(k, y_):
        copies.append(pltpu.make_async_remote_copy(
            src_ref=chunk_of(y_), dst_ref=chunk_of(y_), send_sem=f_send.at[k], recv_sem=f_recv.at[k],
            device_id=mate, device_id_type=MESH,
        ))
        copies[-1].start()

    fin[pl.ds(core * count + y * chunk, chunk)] = value
    for k, peer in y_peers:
        copies.append(pltpu.make_async_remote_copy(
            src_ref=chunk_of(y), dst_ref=chunk_of(y), send_sem=g_send.at[k], recv_sem=g_recv.at[k],
            device_id=peer, device_id_type=MESH,
        ))
        copies[-1].start()
    pass_on(0, y)
    for k in reversed(far_first(ny)):
        source = lax.rem(y + ny - k, ny)
        pltpu.make_async_copy(chunk_of(source), chunk_of(source), g_recv.at[k]).wait()
        pass_on(k, source)
    for k in range(ny):
        source = lax.rem(y + ny - k, ny)
        theirs = fin.at[pl.ds((1 - core) * count + source * chunk, chunk)]
        pltpu.make_async_copy(theirs, theirs, f_recv.at[k]).wait()
    gram_ref[...] = fin[...]

    for copy in copies:
        copy.wait_send()

    @pl.when(has_low)
    def _():
        for q in range(REACH):
            to_low(q).wait_send()

    @pl.when(has_high)
    def _():
        for q in range(REACH):
            to_high(q).wait_send()

    for j in range(LINES):
        pltpu.make_async_copy(high_v.at[j], high_hbm.at[j], store_sem.at[j]).wait()
        pltpu.make_async_copy(low_v.at[j], low_hbm.at[j], store_sem.at[LINES + j]).wait()


def front(sizes, sketch, marginal_std, cov_tiles, tile_cols):
    rows, k = sketch.shape
    tile = cov_tiles.shape[1]
    ny, nx, nz = sizes["ny"], sizes["nx"], sizes["nzh"] * sizes["nzl"]
    total = rows * sizes["nx"] * ny * nz * 2
    count = 24
    chunk = count // ny
    vmem, dma = pltpu.VMEM, pltpu.SemaphoreType.DMA
    block = (LINES, tile, k)
    scratch = [
        vmem(block, BF16), vmem(cov_tiles.shape, BF16), vmem((2 * REACH + LINES, tile, k), BF16),
        vmem((REACH, tile, k), BF16), vmem((REACH, tile, k), BF16),
        vmem((16, 128), F32), vmem((128, 16), F32), vmem(block, F32), vmem(block, BF16), vmem(block, BF16),
        vmem((k, 2 * k), F32),
        vmem((2 * count, 8, 128), F32), vmem((count, 8, 128), F32), vmem((count, 8, 128), F32),
        vmem((ny, chunk, 8, 128), F32), vmem((chunk, 8, 128), F32), vmem((nz, chunk, 8, 128), F32),
        vmem((chunk, 8, 128), F32), vmem((nx, chunk, 8, 128), F32), vmem((2 * count, 8, 128), F32),
        dma((2,)), dma((2 * LINES,)), dma((2 * REACH,)), dma((2 * REACH,)), dma((1,)), dma((1,)),
        dma((ny,)), dma((ny,)), dma((nz,)), dma((nz,)), dma((nx,)), dma((nx,)),
        dma((ny,)), dma((ny,)), dma((ny,)), dma((ny,)),
    ]
    anywhere = pl.BlockSpec(memory_space=pl.ANY)
    return pl.pallas_call(
        functools.partial(front_kernel, sizes, 1.0 / total),
        out_shape=(
            jax.ShapeDtypeStruct(block, BF16), jax.ShapeDtypeStruct(block, BF16),
            jax.ShapeDtypeStruct((2 * count, 8, 128), F32),
        ),
        in_specs=[pl.BlockSpec(memory_space=pltpu.SMEM), pl.BlockSpec(memory_space=pltpu.VMEM), anywhere, anywhere],
        out_specs=(anywhere, anywhere, pl.BlockSpec(memory_space=pltpu.VMEM)),
        scratch_shapes=scratch,
        compiler_params=pltpu.CompilerParams(collective_id=0, has_side_effects=True, vmem_limit_bytes=48 * 2**20),
        name="front",
    )(tile_cols, marginal_std.reshape(LINES, 2, 128), sketch.reshape(block), cov_tiles)


def split3(a):
    a1 = a.astype(BF16)
    rest = a - a1.astype(F32)
    a2 = rest.astype(BF16)
    return a1, a2, (rest - a2.astype(F32)).astype(BF16)


def factor_in_place(work, rows_w, rows_f, n):
    def panel(p, carry):
        lane = lax.broadcasted_iota(jnp.int32, (8, 128), 1)
        sub = lax.broadcasted_iota(jnp.int32, (8, 128), 0)
        groups = PANEL // 8
        left = [work[8 * g : 8 * g + 8, 0:128] for g in range(groups)]
        right = [work[8 * g : 8 * g + 8, 128:n] for g in range(groups)]
        for m in range(PANEL // PIVOT):
            c0 = m * PIVOT
            g0, s0 = c0 // 8, c0 % 8
            inside = (lane >= c0) & (lane < c0 + PIVOT)
            cols = [[jnp.broadcast_to(left[g][:, c0 + q : c0 + q + 1], (8, 128)) for q in range(PIVOT)]
                    for g in range(g0, groups)]
            pick = lambda r, q: jnp.broadcast_to(cols[0][q][s0 + r : s0 + r + 1, :], (8, 128))
            piv = {(r, q): pick(r, q) for q in range(PIVOT) for r in range(q, PIVOT)}
            row_l = [jnp.broadcast_to(left[g0][s0 + q : s0 + q + 1, :], (8, 128)) for q in range(PIVOT)]
            row_r = [jnp.broadcast_to(right[g0][s0 + q : s0 + q + 1, :], (8, 128)) for q in range(PIVOT)]
            row_l = [jnp.where(inside, jnp.where(lane == c0 + q, 1.0, 0.0), row_l[q]) for q in range(PIVOT)]
            u = {}
            inv = []
            for q in range(PIVOT):
                d = piv[q, q]
                i = lax.rsqrt(d)
                inv.append(i)
                u[q, q] = d * i
                for r in range(q + 1, PIVOT):
                    u[q, r] = piv[r, q] * i
                for r in range(q + 1, PIVOT):
                    for t in range(r, PIVOT):
                        piv[t, r] = piv[t, r] - u[q, r] * u[q, t]

            def sweep(v):
                out = []
                for q in range(PIVOT):
                    a = v[q]
                    for r in range(q):
                        a = a - u[r, q] * out[r]
                    out.append(a * inv[q])
                return out

            z_l, z_r = sweep(row_l), sweep(row_r)
            for q in range(PIVOT):
                row = pl.ds(c0 + q, 1)
                rows_w[p, row, 0:128] = z_l[q][0:1]
                rows_w[p, row, 128:n] = z_r[q][0:1]
                f = jnp.where(inside, 0.0, z_l[q])
                for r in range(q, PIVOT):
                    f = jnp.where(lane == c0 + r, u[q, r], f)
                rows_f[p, row, 0:128] = f[0:1]
                rows_f[p, row, 128:n] = z_r[q][0:1]
            for g in range(g0, groups):
                if g == g0 and s0 + PIVOT == 8:
                    continue
                w = sweep(cols[g - g0])
                if g == g0:
                    w = [jnp.where(sub >= s0 + PIVOT, v, 0.0) for v in w]
                cleared = jnp.where(inside & (sub >= s0 + PIVOT) if g == g0 else inside, 0.0, left[g])
                for q in range(PIVOT):
                    cleared = cleared - w[q] * z_l[q]
                    right[g] = right[g] - w[q] * z_r[q]
                left[g] = cleared

        at = lax.broadcasted_iota(jnp.int32, (PANEL, n), 1)
        below_diagonal = at <= lax.broadcasted_iota(jnp.int32, (PANEL, n), 0)
        b1, b2, b3 = split3(jnp.where(below_diagonal | (at >= PANEL), rows_w[p], 0.0))
        lhs = jnp.concatenate([b1, b1, b2, b2, b1, b3], axis=0)
        rhs = jnp.concatenate([b1, b2, b1, b2, b3, b1], axis=0)
        update = lax.dot_general(lhs, rhs, (((0,), (0,)), ((), ())), preferred_element_type=F32)
        lanes = lax.broadcasted_iota(jnp.int32, (n - PANEL, n), 1)
        fresh = jnp.where(lanes < PANEL, 0.0, work[PANEL:, :]) - update[PANEL:, :]
        work[0 : n - PANEL, :] = pltpu.roll(fresh, n - PANEL, 1)
        return carry

    lax.fori_loop(0, n // PANEL, panel, 0)


def back_kernel(cols_ref, gram_ref, high_hbm, low_hbm, basis_hbm, factor_ref,
                high_v, low_v, out_v, work, rows_w, rows_f, w_high, w_low, load_sem, out_sem):
    n = work.shape[0]
    half = n // 2
    loads = [
        pltpu.make_async_copy(high_hbm, high_v, load_sem.at[0]),
        pltpu.make_async_copy(low_hbm, low_v, load_sem.at[1]),
    ]
    for copy in loads:
        copy.start()
    upper = gram_ref[16:32].reshape(half, half)
    work[0:half, 0:half] = gram_ref[0:16].reshape(half, half)
    work[0:half, half:] = upper
    work[half:, 0:half] = upper.T
    work[half:, half:] = gram_ref[32:48].reshape(half, half)
    factor_in_place(work, rows_w, rows_f, n)

    for p in range(n // PANEL):
        rows = slice(p * PANEL, p * PANEL + PANEL)
        row = lax.broadcasted_iota(jnp.int32, (PANEL, n), 0) + p * PANEL
        col = lax.broadcasted_iota(jnp.int32, (PANEL, n), 1)
        w, f = rows_w[p], rows_f[p]
        if p:
            w, f = pltpu.roll(w, p * PANEL, 1), pltpu.roll(f, p * PANEL, 1)
        w = jnp.where(col <= row, w, 0.0)
        factor_ref[rows, :] = jnp.where(col >= row, f, 0.0)
        high = w.astype(BF16)
        w_high[rows, :] = high
        w_low[rows, :] = (w - high.astype(F32)).astype(BF16)

    for copy in loads:
        copy.wait()
    wh, wl = w_high[...], w_low[...]
    weights = jnp.concatenate([wh, wl, wh], axis=1)
    writes = []
    for t in range(LINES):
        head = t // REACH * REACH
        start = cols_ref[head, REACH]
        start = start - start % REACH
        line = jnp.int32(head)
        for e in range(REACH):
            line += jnp.where(cols_ref[t, e] >= start, 1, 0)
        line = jnp.clip(line, 0, LINES - 1)
        h, l = high_v[line], low_v[line]
        out_v[t] = lax.dot_general(
            jnp.concatenate([h, h, l], axis=1), weights, (((1,), (1,)), ((), ())), preferred_element_type=F32
        )
        writes.append(pltpu.make_async_copy(out_v.at[t], basis_hbm.at[t], out_sem.at[t]))
        writes[-1].start()
    for copy in writes:
        copy.wait()


def back(tile_cols, gram, high, low):
    lines, tile, k = high.shape
    vmem, dma = pltpu.VMEM, pltpu.SemaphoreType.DMA
    anywhere = pl.BlockSpec(memory_space=pl.ANY)
    in_vmem = pl.BlockSpec(memory_space=pltpu.VMEM)
    return pl.pallas_call(
        back_kernel,
        out_shape=(jax.ShapeDtypeStruct((lines, tile, k), F32), jax.ShapeDtypeStruct((k, k), F32)),
        in_specs=[pl.BlockSpec(memory_space=pltpu.SMEM), in_vmem, anywhere, anywhere],
        out_specs=(anywhere, in_vmem),
        scratch_shapes=[
            vmem((lines, tile, k), BF16), vmem((lines, tile, k), BF16), vmem((lines, tile, k), F32),
            vmem((k, k), F32), vmem((k // PANEL, PANEL, k), F32), vmem((k // PANEL, PANEL, k), F32),
            vmem((k, k), BF16), vmem((k, k), BF16), dma((2,)), dma((lines,)),
        ],
        compiler_params=pltpu.CompilerParams(vmem_limit_bytes=48 * 2**20),
        name="back",
    )(tile_cols, gram, high, low)


def per_device(sizes, sketch, marginal_std, cov_tiles, tile_cols):
    high, low, gram = front(sizes, sketch, marginal_std, cov_tiles, tile_cols)
    basis, factor = back(tile_cols, gram, high, low)
    return basis.reshape(sketch.shape), factor


def build(mesh, sizes):
    in_specs = (P(("grp", "dev"), None), P(("grp", "dev")), P(), P(("grp", "dev"), None))
    out_specs = (P(("grp", "dev"), None), P())
    return jax.shard_map(
        functools.partial(per_device, sizes), mesh=mesh, in_specs=in_specs, out_specs=out_specs, check_vma=False
    )


def solution(mesh):
    return build(mesh, SIZES)
```

```python
import functools

import jax
import jax.numpy as jnp
from jax import lax
from jax.experimental import pallas as pl
from jax.experimental.pallas import tpu as pltpu
from jax.sharding import PartitionSpec as P

MESH = pl.DeviceIdType.MESH
F32, BF16 = jnp.float32, jnp.bfloat16
REACH = 4
LINES = 8
LAGS = 9
PANEL = 32
PIVOT = 8

SIZES = dict(nx=4, ny=8, nzh=4, nzl=2)


def pin_hbm(a):
    return pltpu.with_memory_space_constraint(a, pltpu.HBM)


def far_first(n):
    return sorted(range(1, n), key=lambda k: -min(k, n - k))


def front_kernel(
    sizes, scale, cols_hbm, std_hbm, sketch_hbm, cov_hbm, high_v, low_v, fin,
    cols_ref, std_ref, sketch_v, cov_v, own, below, above, std_sorted, std_cols, acc, gacc,
    packed, from_core, part, got_a, sum_a, got_b, sum_b, got_x,
    load_sem, halo_send, halo_recv, core_send, core_recv, a_send, a_recv,
    b_send, b_recv, x_send, x_recv, g_send, g_recv, f_send, f_recv,
):
    nx, ny, nzh, nzl = sizes["nx"], sizes["ny"], sizes["nzh"], sizes["nzl"]
    nz = nzh * nzl
    grp, dev = lax.axis_index("grp"), lax.axis_index("dev")
    per_grp = nx * nzh * 2
    total = per_grp * ny * nzl
    me = grp * per_grp + dev
    y, z_lo = lax.rem(grp, ny), lax.div(grp, ny)
    core = lax.rem(dev, 2)
    z_hi, x = lax.rem(lax.div(dev, 2), nzh), lax.div(dev, 2 * nzh)
    z = z_hi * nzl + z_lo

    def place(x_, y_, z_, core_):
        return (lax.rem(z_, nzl) * ny + y_, (x_ * nzh + lax.div(z_, nzl)) * 2 + core_)

    def linear(i):
        return (lax.div(i, per_grp), lax.rem(i, per_grp))

    mate = place(x, y, z, 1 - core)
    outer = jnp.where(core == 0, me - 1, me + 1)
    has_outer = (outer >= 0) & (outer < total)
    has_low, has_high = me > 0, me < total - 1

    load_cols = pltpu.make_async_copy(cols_hbm, cols_ref, load_sem.at[0])
    load_std = pltpu.make_async_copy(std_hbm, std_ref, load_sem.at[1])
    load_sketch = pltpu.make_async_copy(sketch_hbm, sketch_v, load_sem.at[2])
    load_cov = pltpu.make_async_copy(cov_hbm, cov_v, load_sem.at[3])
    for copy in (load_cols, load_std, load_sketch, load_cov):
        copy.start()

    barrier = pltpu.get_barrier_semaphore()

    def greet(device):
        pl.semaphore_signal(barrier, inc=1, device_id=device, device_id_type=MESH)

    y_peers = [(k, place(x, lax.rem(y + k, ny), z, core)) for k in far_first(ny)]
    z_peers = [(k, place(x, y, lax.rem(z + k, nz), core)) for k in far_first(nz)]
    x_peers = [(k, place(lax.rem(x + k, nx), y, z, core)) for k in far_first(nx)]
    for _, peer in z_peers + y_peers + x_peers:
        greet(peer)
    greet(mate)

    @pl.when(has_outer)
    def _():
        greet(linear(outer))

    gacc[...] = jnp.zeros_like(gacc)
    zero_lines = jnp.zeros((REACH,) + own.shape[1:], BF16)
    own[0:REACH] = zero_lines
    own[REACH + LINES :] = zero_lines

    @pl.when(jnp.logical_not(has_low))
    def _():
        below[...] = zero_lines

    @pl.when(jnp.logical_not(has_high))
    def _():
        above[...] = zero_lines

    load_cols.wait()
    tile_of_line = []
    for block in range(LINES // REACH):
        head = block * REACH
        start = cols_ref[head, REACH]
        offset = jnp.int32(0)
        for e in range(REACH):
            offset += jnp.where(cols_ref[head, e] >= start, 1, 0)
        for j in range(REACH):
            tile = cols_ref[head, REACH - offset + j] - start
            tile_of_line.append(jnp.clip(tile, 0, REACH - 1) + head)

    load_std.wait()
    for j in range(LINES):
        std_sorted[2 * j : 2 * j + 2, :] = std_ref[tile_of_line[j]]
    std_cols[...] = std_sorted[...].T

    def std_of(j):
        return jnp.concatenate([std_cols[:, 2 * j : 2 * j + 1], std_cols[:, 2 * j + 1 : 2 * j + 2]], axis=0)

    load_sketch.wait()
    for j in (0, 7, 1, 6, 2, 5, 3, 4):
        own[REACH + j] = (sketch_v[tile_of_line[j]].astype(F32) * std_of(j)).astype(BF16)

    n, a_at, b_at = ny, jnp.where(core == 0, y, z), jnp.where(core == 0, z, y)

    def cross(first, second):
        return [
            (k, tuple(jnp.where(core == 0, p, q) for p, q in zip(one, two)))
            for (k, one), (_, two) in zip(first, second)
        ]

    a_peers, b_peers = cross(y_peers, z_peers), cross(z_peers, y_peers)

    peers = len(y_peers) + len(z_peers) + len(x_peers) + 1
    pl.semaphore_wait(barrier, peers + jnp.where(has_outer, 1, 0))

    def to_low(q):
        return pltpu.make_async_remote_copy(
            src_ref=own.at[REACH + q], dst_ref=above.at[q], send_sem=halo_send.at[q],
            recv_sem=halo_recv.at[q], device_id=linear(me - 1), device_id_type=MESH,
        )

    def to_high(q):
        return pltpu.make_async_remote_copy(
            src_ref=own.at[REACH + LINES - 1 - q], dst_ref=below.at[q], send_sem=halo_send.at[REACH + q],
            recv_sem=halo_recv.at[REACH + q], device_id=linear(me + 1), device_id_type=MESH,
        )

    @pl.when(has_low)
    def _():
        for q in range(REACH):
            to_low(q).start()

    @pl.when(has_high)
    def _():
        for q in range(REACH):
            to_high(q).start()

    load_cov.wait()

    def own_line(j, carry):
        lags = jnp.concatenate([cov_v[e] for e in range(LAGS)], axis=1)
        lines = own[pl.ds(j, LAGS)].reshape(LAGS * own.shape[1], own.shape[2])
        acc[j] = jnp.dot(lags, lines, preferred_element_type=F32)
        return carry

    lax.fori_loop(0, LINES, own_line, 0)

    def finish(j, product):
        latent = product * std_of(j)
        high = latent.astype(BF16)
        low = (latent - high.astype(F32)).astype(BF16)
        high_v[j] = high
        low_v[j] = low
        pair = jnp.concatenate([high, low], axis=1)
        gacc[...] += lax.dot_general(high, pair, (((0,), (0,)), ((), ())), preferred_element_type=F32)

    for q in range(REACH):
        @pl.when(has_low)
        def _():
            to_high(q).wait_recv()

        for j in range(REACH - q):
            e = (-1 - q) - j + REACH
            product = acc[j] + jnp.dot(cov_v[e], below[q], preferred_element_type=F32)
            if j == REACH - 1 - q:
                finish(j, product)
            else:
                acc[j] = product

        @pl.when(has_high)
        def _():
            to_low(q).wait_recv()

        for j in range(REACH + q, LINES):
            e = (LINES + q) - j + REACH
            product = acc[j] + jnp.dot(cov_v[e], above[q], preferred_element_type=F32)
            if j == REACH + q:
                finish(j, product)
            else:
                acc[j] = product

    half = gacc.shape[0] // 2
    for block, (r, c) in enumerate(((0, 0), (0, half), (half, half))):
        hh = gacc[r : r + half, c : c + half]
        hl = gacc[r : r + half, 2 * half + c : 3 * half + c]
        lh = gacc[c : c + half, 2 * half + r : 3 * half + r].T
        packed[16 * block : 16 * block + 16] = ((hh + (hl + lh)) * scale).reshape(16, 8, 128)

    count = packed.shape[0] // 2
    chunk = count // ny
    swap = pltpu.make_async_remote_copy(
        src_ref=packed.at[pl.ds((1 - core) * count, count)], dst_ref=from_core, send_sem=core_send.at[0],
        recv_sem=core_recv.at[0], device_id=mate, device_id_type=MESH,
    )
    swap.start()
    swap.wait()
    part[...] = packed[pl.ds(core * count, count)] + from_core[...]

    copies = []
    for k, peer in a_peers:
        copies.append(pltpu.make_async_remote_copy(
            src_ref=part.at[pl.ds(lax.rem(a_at + k, n) * chunk, chunk)], dst_ref=got_a.at[k],
            send_sem=a_send.at[k], recv_sem=a_recv.at[k], device_id=peer, device_id_type=MESH,
        ))
        copies[-1].start()
    value = part[pl.ds(a_at * chunk, chunk)]
    for k in reversed(far_first(n)):
        pltpu.make_async_copy(got_a.at[k], got_a.at[k], a_recv.at[k]).wait()
        value = value + got_a[k]

    def gather_sum(value, here, n, peers_, source, slots, send, recv):
        source[...] = value
        for k, peer in peers_:
            copies.append(pltpu.make_async_remote_copy(
                src_ref=source, dst_ref=slots.at[here], send_sem=send.at[k], recv_sem=recv.at[k],
                device_id=peer, device_id_type=MESH,
            ))
            copies[-1].start()
        slots[pl.ds(here, 1)] = value[None]
        for k in range(1, n):
            pltpu.make_async_copy(source, source, recv.at[k]).wait()
        out = slots[0]
        for i in range(1, n):
            out = out + slots[i]
        return out

    value = gather_sum(value, b_at, n, b_peers, sum_a, got_b, b_send, b_recv)
    value = gather_sum(value, x, nx, x_peers, sum_b, got_x, x_send, x_recv)

    def chunk_of(a_):
        return fin.at[pl.ds(core * count + a_ * chunk, chunk)]

    def pass_on(k, a_):
        copies.append(pltpu.make_async_remote_copy(
            src_ref=chunk_of(a_), dst_ref=chunk_of(a_), send_sem=f_send.at[k], recv_sem=f_recv.at[k],
            device_id=mate, device_id_type=MESH,
        ))
        copies[-1].start()

    fin[pl.ds(core * count + a_at * chunk, chunk)] = value
    for k, peer in a_peers:
        copies.append(pltpu.make_async_remote_copy(
            src_ref=chunk_of(a_at), dst_ref=chunk_of(a_at), send_sem=g_send.at[k], recv_sem=g_recv.at[k],
            device_id=peer, device_id_type=MESH,
        ))
        copies[-1].start()
    pass_on(0, a_at)
    for k in reversed(far_first(n)):
        source = lax.rem(a_at + n - k, n)
        pltpu.make_async_copy(chunk_of(source), chunk_of(source), g_recv.at[k]).wait()
        pass_on(k, source)
    for k in range(n):
        source = lax.rem(b_at + n - k, n)
        theirs = fin.at[pl.ds((1 - core) * count + source * chunk, chunk)]
        pltpu.make_async_copy(theirs, theirs, f_recv.at[k]).wait()
    for copy in copies:
        copy.wait_send()

    @pl.when(has_low)
    def _():
        for q in range(REACH):
            to_low(q).wait_send()

    @pl.when(has_high)
    def _():
        for q in range(REACH):
            to_high(q).wait_send()


def front(sizes, sketch, marginal_std, cov_tiles, tile_cols):
    rows, k = sketch.shape
    tile = cov_tiles.shape[1]
    ny, nx, nz = sizes["ny"], sizes["nx"], sizes["nzh"] * sizes["nzl"]
    total = rows * sizes["nx"] * ny * nz * 2
    count = 24
    chunk = count // ny
    vmem, dma = pltpu.VMEM, pltpu.SemaphoreType.DMA
    block = (LINES, tile, k)
    scratch = [
        pltpu.SMEM(tile_cols.shape, jnp.int32), vmem((LINES, 2, 128), F32), vmem(block, BF16), vmem(cov_tiles.shape, BF16), vmem((2 * REACH + LINES, tile, k), BF16),
        vmem((REACH, tile, k), BF16), vmem((REACH, tile, k), BF16),
        vmem((16, 128), F32), vmem((128, 16), F32), vmem(block, F32),
        vmem((k, 2 * k), F32),
        vmem((2 * count, 8, 128), F32), vmem((count, 8, 128), F32), vmem((count, 8, 128), F32),
        vmem((ny, chunk, 8, 128), F32), vmem((chunk, 8, 128), F32), vmem((nz, chunk, 8, 128), F32),
        vmem((chunk, 8, 128), F32), vmem((nx, chunk, 8, 128), F32),
        dma((4,)), dma((2 * REACH,)), dma((2 * REACH,)), dma((1,)), dma((1,)),
        dma((ny,)), dma((ny,)), dma((nz,)), dma((nz,)), dma((nx,)), dma((nx,)),
        dma((ny,)), dma((ny,)), dma((ny,)), dma((ny,)),
    ]
    in_hbm = pl.BlockSpec(memory_space=pltpu.HBM)
    in_vmem = pl.BlockSpec(memory_space=pltpu.VMEM)
    return pl.pallas_call(
        functools.partial(front_kernel, sizes, 1.0 / total),
        out_shape=(
            jax.ShapeDtypeStruct(block, BF16), jax.ShapeDtypeStruct(block, BF16),
            jax.ShapeDtypeStruct((2 * count, 8, 128), F32),
        ),
        in_specs=[in_hbm] * 4,
        out_specs=(in_vmem,) * 3,
        scratch_shapes=scratch,
        compiler_params=pltpu.CompilerParams(collective_id=0, has_side_effects=True, vmem_limit_bytes=48 * 2**20),
        name="front",
    )(*(pin_hbm(a) for a in (tile_cols, marginal_std.reshape(LINES, 2, 128), sketch.reshape(block), cov_tiles)))


def split3(a):
    a1 = a.astype(BF16)
    rest = a - a1.astype(F32)
    a2 = rest.astype(BF16)
    return a1, a2, (rest - a2.astype(F32)).astype(BF16)


def factor_in_place(work, rows_w, rows_f, n):
    def panel(p, carry):
        lane = lax.broadcasted_iota(jnp.int32, (8, 128), 1)
        sub = lax.broadcasted_iota(jnp.int32, (8, 128), 0)
        groups = PANEL // 8
        left = [work[8 * g : 8 * g + 8, 0:128] for g in range(groups)]
        right = [work[8 * g : 8 * g + 8, 128:n] for g in range(groups)]
        for m in range(PANEL // PIVOT):
            c0 = m * PIVOT
            g0, s0 = c0 // 8, c0 % 8
            inside = (lane >= c0) & (lane < c0 + PIVOT)
            cols = [[jnp.broadcast_to(left[g][:, c0 + q : c0 + q + 1], (8, 128)) for q in range(PIVOT)]
                    for g in range(g0, groups)]
            pick = lambda r, q: jnp.broadcast_to(cols[0][q][s0 + r : s0 + r + 1, :], (8, 128))
            piv = {(r, q): pick(r, q) for q in range(PIVOT) for r in range(q, PIVOT)}
            row_l = [jnp.broadcast_to(left[g0][s0 + q : s0 + q + 1, :], (8, 128)) for q in range(PIVOT)]
            row_r = [jnp.broadcast_to(right[g0][s0 + q : s0 + q + 1, :], (8, 128)) for q in range(PIVOT)]
            row_l = [jnp.where(inside, jnp.where(lane == c0 + q, 1.0, 0.0), row_l[q]) for q in range(PIVOT)]
            u = {}
            inv = []
            for q in range(PIVOT):
                d = piv[q, q]
                i = lax.rsqrt(d)
                inv.append(i)
                u[q, q] = d * i
                for r in range(q + 1, PIVOT):
                    u[q, r] = piv[r, q] * i
                for r in range(q + 1, PIVOT):
                    for t in range(r, PIVOT):
                        piv[t, r] = piv[t, r] - u[q, r] * u[q, t]

            def sweep(v):
                out = []
                for q in range(PIVOT):
                    a = v[q]
                    for r in range(q):
                        a = a - u[r, q] * out[r]
                    out.append(a * inv[q])
                return out

            z_l, z_r = sweep(row_l), sweep(row_r)
            for q in range(PIVOT):
                row = pl.ds(c0 + q, 1)
                rows_w[p, row, 0:128] = z_l[q][0:1]
                rows_w[p, row, 128:n] = z_r[q][0:1]
                f = jnp.where(inside, 0.0, z_l[q])
                for r in range(q, PIVOT):
                    f = jnp.where(lane == c0 + r, u[q, r], f)
                rows_f[p, row, 0:128] = f[0:1]
                rows_f[p, row, 128:n] = z_r[q][0:1]
            for g in range(g0, groups):
                if g == g0 and s0 + PIVOT == 8:
                    continue
                w = sweep(cols[g - g0])
                if g == g0:
                    w = [jnp.where(sub >= s0 + PIVOT, v, 0.0) for v in w]
                cleared = jnp.where(inside & (sub >= s0 + PIVOT) if g == g0 else inside, 0.0, left[g])
                for q in range(PIVOT):
                    cleared = cleared - w[q] * z_l[q]
                    right[g] = right[g] - w[q] * z_r[q]
                left[g] = cleared

        at = lax.broadcasted_iota(jnp.int32, (PANEL, n), 1)
        below_diagonal = at <= lax.broadcasted_iota(jnp.int32, (PANEL, n), 0)
        b1, b2, b3 = split3(jnp.where(below_diagonal | (at >= PANEL), rows_w[p], 0.0))
        lhs = jnp.concatenate([b1, b1, b2, b2, b1, b3], axis=0)
        rhs = jnp.concatenate([b1, b2, b1, b2, b3, b1], axis=0)
        update = lax.dot_general(lhs, rhs, (((0,), (0,)), ((), ())), preferred_element_type=F32)
        lanes = lax.broadcasted_iota(jnp.int32, (n - PANEL, n), 1)
        fresh = jnp.where(lanes < PANEL, 0.0, work[PANEL:, :]) - update[PANEL:, :]
        work[0 : n - PANEL, :] = pltpu.roll(fresh, n - PANEL, 1)
        return carry

    lax.fori_loop(0, n // PANEL, panel, 0)


def back_kernel(cols_hbm, gram_ref, high_v, low_v, basis_hbm, factor_ref,
                cols_ref, out_v, work, rows_w, rows_f, w_high, w_low, load_sem, out_sem):
    n = work.shape[0]
    half = n // 2
    load_cols = pltpu.make_async_copy(cols_hbm, cols_ref, load_sem.at[0])
    load_cols.start()
    upper = gram_ref[16:32].reshape(half, half)
    work[0:half, 0:half] = gram_ref[0:16].reshape(half, half)
    work[0:half, half:] = upper
    work[half:, 0:half] = upper.T
    work[half:, half:] = gram_ref[32:48].reshape(half, half)
    factor_in_place(work, rows_w, rows_f, n)

    for p in range(n // PANEL):
        rows = slice(p * PANEL, p * PANEL + PANEL)
        row = lax.broadcasted_iota(jnp.int32, (PANEL, n), 0) + p * PANEL
        col = lax.broadcasted_iota(jnp.int32, (PANEL, n), 1)
        w, f = rows_w[p], rows_f[p]
        if p:
            w, f = pltpu.roll(w, p * PANEL, 1), pltpu.roll(f, p * PANEL, 1)
        w = jnp.where(col <= row, w, 0.0)
        factor_ref[rows, :] = jnp.where(col >= row, f, 0.0)
        high = w.astype(BF16)
        w_high[rows, :] = high
        w_low[rows, :] = (w - high.astype(F32)).astype(BF16)

    load_cols.wait()
    wh, wl = w_high[...], w_low[...]
    weights = jnp.concatenate([wh, wl, wh], axis=1)
    writes = []
    for t in range(LINES):
        head = t // REACH * REACH
        start = cols_ref[head, REACH]
        start = start - start % REACH
        line = jnp.int32(head)
        for e in range(REACH):
            line += jnp.where(cols_ref[t, e] >= start, 1, 0)
        line = jnp.clip(line, 0, LINES - 1)
        h, l = high_v[line], low_v[line]
        out_v[t] = lax.dot_general(
            jnp.concatenate([h, h, l], axis=1), weights, (((1,), (1,)), ((), ())), preferred_element_type=F32
        )
        writes.append(pltpu.make_async_copy(out_v.at[t], basis_hbm.at[t], out_sem.at[t]))
        writes[-1].start()
    for copy in writes:
        copy.wait()


def back(tile_cols, gram, high, low):
    lines, tile, k = high.shape
    vmem, dma = pltpu.VMEM, pltpu.SemaphoreType.DMA
    in_hbm = pl.BlockSpec(memory_space=pltpu.HBM)
    in_vmem = pl.BlockSpec(memory_space=pltpu.VMEM)
    return pl.pallas_call(
        back_kernel,
        out_shape=(jax.ShapeDtypeStruct((lines, tile, k), F32), jax.ShapeDtypeStruct((k, k), F32)),
        in_specs=[in_hbm, in_vmem, in_vmem, in_vmem],
        out_specs=(in_hbm, in_vmem),
        scratch_shapes=[
            pltpu.SMEM(tile_cols.shape, jnp.int32), vmem((lines, tile, k), F32),
            vmem((k, k), F32), vmem((k // PANEL, PANEL, k), F32), vmem((k // PANEL, PANEL, k), F32),
            vmem((k, k), BF16), vmem((k, k), BF16), dma((1,)), dma((lines,)),
        ],
        compiler_params=pltpu.CompilerParams(vmem_limit_bytes=48 * 2**20),
        name="back",
    )(pin_hbm(tile_cols), gram, high, low)


def per_device(sizes, sketch, marginal_std, cov_tiles, tile_cols):
    high, low, gram = front(sizes, sketch, marginal_std, cov_tiles, tile_cols)
    basis, factor = back(tile_cols, gram, high, low)
    return basis.reshape(sketch.shape), factor


def build(mesh, sizes):
    in_specs = (P(("grp", "dev"), None), P(("grp", "dev")), P(), P(("grp", "dev"), None))
    out_specs = (P(("grp", "dev"), None), P())
    return jax.shard_map(
        functools.partial(per_device, sizes), mesh=mesh, in_specs=in_specs, out_specs=out_specs, check_vma=False
    )


def solution(mesh):
    return build(mesh, SIZES)
```

```python
import functools

import jax
import jax.numpy as jnp
from jax import lax
from jax.experimental import pallas as pl
from jax.experimental.pallas import tpu as pltpu
from jax.sharding import PartitionSpec as P

MESH = pl.DeviceIdType.MESH
F32, BF16 = jnp.float32, jnp.bfloat16
REACH = 4
LINES = 8
LAGS = 9
PANEL = 32
PIVOT = 8

SIZES = dict(nx=4, ny=8, nzh=4, nzl=2)


def pin_hbm(a):
    return pltpu.with_memory_space_constraint(a, pltpu.HBM)


def far_first(n):
    return sorted(range(1, n), key=lambda k: -min(k, n - k))


def front_kernel(
    sizes, scale, cols_hbm, std_hbm, sketch_hbm, cov_hbm, high_v, low_v, fin,
    cols_ref, std_ref, sketch_v, cov_v, own, below, above, std_sorted, std_cols, acc, gacc,
    packed, got_a, sum_a, got_b, sum_b, got_x,
    load_sem, halo_send, halo_recv, a_send, a_recv,
    b_send, b_recv, x_send, x_recv, g_send, g_recv,
):
    nx, ny, nzh, nzl = sizes["nx"], sizes["ny"], sizes["nzh"], sizes["nzl"]
    nz = nzh * nzl
    grp, dev = lax.axis_index("grp"), lax.axis_index("dev")
    per_grp = nx * nzh * 2
    total = per_grp * ny * nzl
    me = grp * per_grp + dev
    y, z_lo = lax.rem(grp, ny), lax.div(grp, ny)
    core = lax.rem(dev, 2)
    z_hi, x = lax.rem(lax.div(dev, 2), nzh), lax.div(dev, 2 * nzh)
    z = z_hi * nzl + z_lo

    def place(x_, y_, z_, core_):
        return (lax.rem(z_, nzl) * ny + y_, (x_ * nzh + lax.div(z_, nzl)) * 2 + core_)

    def linear(i):
        return (lax.div(i, per_grp), lax.rem(i, per_grp))

    outer = jnp.where(core == 0, me - 1, me + 1)
    has_outer = (outer >= 0) & (outer < total)
    has_low, has_high = me > 0, me < total - 1

    load_cols = pltpu.make_async_copy(cols_hbm, cols_ref, load_sem.at[0])
    load_std = pltpu.make_async_copy(std_hbm, std_ref, load_sem.at[1])
    load_sketch = pltpu.make_async_copy(sketch_hbm, sketch_v, load_sem.at[2])
    load_cov = pltpu.make_async_copy(cov_hbm, cov_v, load_sem.at[3])
    for copy in (load_cols, load_std, load_sketch, load_cov):
        copy.start()

    barrier = pltpu.get_barrier_semaphore()

    def greet(device):
        pl.semaphore_signal(barrier, inc=1, device_id=device, device_id_type=MESH)

    y_peers = [(k, place(x, lax.rem(y + k, ny), z, core)) for k in far_first(ny)]
    z_peers = [(k, place(x, y, lax.rem(z + k, nz), core)) for k in far_first(nz)]
    x_peers = [(k, place(lax.rem(x + k, nx), y, z, core)) for k in far_first(nx)]
    y_across = [(k, place(x, lax.rem(y + k, ny), z, 1 - core)) for k in far_first(ny) + [0]]
    z_across = [(k, place(x, y, lax.rem(z + k, nz), 1 - core)) for k in far_first(nz) + [0]]
    for _, peer in z_peers + y_peers + x_peers + y_across + z_across[:-1]:
        greet(peer)

    @pl.when(has_outer)
    def _():
        greet(linear(outer))

    gacc[...] = jnp.zeros_like(gacc)
    zero_lines = jnp.zeros((REACH,) + own.shape[1:], BF16)
    own[0:REACH] = zero_lines
    own[REACH + LINES :] = zero_lines

    @pl.when(jnp.logical_not(has_low))
    def _():
        below[...] = zero_lines

    @pl.when(jnp.logical_not(has_high))
    def _():
        above[...] = zero_lines

    load_cols.wait()
    tile_of_line = []
    for block in range(LINES // REACH):
        head = block * REACH
        start = cols_ref[head, REACH]
        offset = jnp.int32(0)
        for e in range(REACH):
            offset += jnp.where(cols_ref[head, e] >= start, 1, 0)
        for j in range(REACH):
            tile = cols_ref[head, REACH - offset + j] - start
            tile_of_line.append(jnp.clip(tile, 0, REACH - 1) + head)

    load_std.wait()
    for j in range(LINES):
        std_sorted[2 * j : 2 * j + 2, :] = std_ref[tile_of_line[j]]
    std_cols[...] = std_sorted[...].T

    def std_of(j):
        return jnp.concatenate([std_cols[:, 2 * j : 2 * j + 1], std_cols[:, 2 * j + 1 : 2 * j + 2]], axis=0)

    def scale_lines(q):
        for j in (q, LINES - 1 - q):
            own[REACH + j] = (sketch_v[tile_of_line[j]].astype(F32) * std_of(j)).astype(BF16)

    load_sketch.wait()
    scale_lines(0)
    scale_lines(1)

    n, a_at, b_at = ny, jnp.where(core == 0, y, z), jnp.where(core == 0, z, y)

    def cross(first, second):
        return [
            (k, tuple(jnp.where(core == 0, p, q) for p, q in zip(one, two)))
            for (k, one), (_, two) in zip(first, second)
        ]

    a_peers, b_peers = cross(y_peers, z_peers), cross(z_peers, y_peers)
    a_across, b_across = cross(y_across, z_across), cross(z_across, y_across)

    peers = len(z_peers + y_peers + x_peers + y_across + z_across) - 1
    pl.semaphore_wait(barrier, peers + jnp.where(has_outer, 1, 0))

    def to_low(q):
        return pltpu.make_async_remote_copy(
            src_ref=own.at[REACH + q], dst_ref=above.at[q], send_sem=halo_send.at[q],
            recv_sem=halo_recv.at[q], device_id=linear(me - 1), device_id_type=MESH,
        )

    def to_high(q):
        return pltpu.make_async_remote_copy(
            src_ref=own.at[REACH + LINES - 1 - q], dst_ref=below.at[q], send_sem=halo_send.at[REACH + q],
            recv_sem=halo_recv.at[REACH + q], device_id=linear(me + 1), device_id_type=MESH,
        )

    for q in range(REACH):
        @pl.when(has_low)
        def _():
            to_low(q).start()

        @pl.when(has_high)
        def _():
            to_high(q).start()

        if q + 2 < REACH:
            scale_lines(q + 2)

    load_cov.wait()

    def own_line(j, carry):
        lags = jnp.concatenate([cov_v[e] for e in range(LAGS)], axis=1)
        lines = own[pl.ds(j, LAGS)].reshape(LAGS * own.shape[1], own.shape[2])
        acc[j] = jnp.dot(lags, lines, preferred_element_type=F32)
        return carry

    lax.fori_loop(0, LINES, own_line, 0)

    def finish(j, product):
        latent = product * std_of(j)
        high = latent.astype(BF16)
        low = (latent - high.astype(F32)).astype(BF16)
        high_v[j] = high
        low_v[j] = low
        pair = jnp.concatenate([high, low], axis=1)
        gacc[...] += lax.dot_general(high, pair, (((0,), (0,)), ((), ())), preferred_element_type=F32)

    for q in range(REACH):
        @pl.when(has_low)
        def _():
            to_high(q).wait_recv()

        for j in range(REACH - q):
            e = (-1 - q) - j + REACH
            product = acc[j] + jnp.dot(cov_v[e], below[q], preferred_element_type=F32)
            if j == REACH - 1 - q:
                finish(j, product)
            else:
                acc[j] = product

        @pl.when(has_high)
        def _():
            to_low(q).wait_recv()

        for j in range(REACH + q, LINES):
            e = (LINES + q) - j + REACH
            product = acc[j] + jnp.dot(cov_v[e], above[q], preferred_element_type=F32)
            if j == REACH + q:
                finish(j, product)
            else:
                acc[j] = product

    half = gacc.shape[0] // 2
    for block, (r, c) in enumerate(((0, 0), (0, half), (half, half))):
        hh = gacc[r : r + half, c : c + half]
        hl = gacc[r : r + half, 2 * half + c : 3 * half + c]
        lh = gacc[c : c + half, 2 * half + r : 3 * half + r].T
        packed[16 * block : 16 * block + 16] = ((hh + (hl + lh)) * scale).reshape(16, 8, 128)

    count = packed.shape[0] // 2
    chunk = count // n
    copies = []

    def send(source, target, send_sem, recv_sem, peer):
        copies.append(pltpu.make_async_remote_copy(
            src_ref=source, dst_ref=target, send_sem=send_sem, recv_sem=recv_sem, device_id=peer, device_id_type=MESH,
        ))
        copies[-1].start()

    def piece(half_of, at):
        return pl.ds(half_of * count + at * chunk, chunk)

    for (k, peer), (_, other) in zip(a_peers + [(0, None)], b_across):
        if k:
            own_piece = packed.at[piece(core, lax.rem(a_at + k, n))]
            send(own_piece, got_a.at[0, k], a_send.at[0, k], a_recv.at[0, k], peer)
        their_piece = packed.at[piece(1 - core, lax.rem(b_at + k, n))]
        send(their_piece, got_a.at[1, k], a_send.at[1, k], a_recv.at[1, k], other)
    value = packed[piece(core, a_at)]
    for k in [0] + far_first(n)[::-1]:
        for side in (0, 1) if k else (1,):
            pltpu.make_async_copy(got_a.at[side, k], got_a.at[side, k], a_recv.at[side, k]).wait()
            value = value + got_a[side, k]

    def gather_sum(value, here, peers_, source, slots, send_sem, recv_sem):
        source[...] = value
        for k, peer in peers_:
            send(source, slots.at[here], send_sem.at[k], recv_sem.at[k], peer)
        slots[pl.ds(here, 1)] = value[None]
        for k in range(1, slots.shape[0]):
            pltpu.make_async_copy(source, source, recv_sem.at[k]).wait()
        out = slots[0]
        for i in range(1, slots.shape[0]):
            out = out + slots[i]
        return out

    value = gather_sum(value, b_at, b_peers, sum_a, got_b, b_send, b_recv)
    value = gather_sum(value, x, x_peers, sum_b, got_x, x_send, x_recv)

    mine = fin.at[piece(core, a_at)]
    fin[piece(core, a_at)] = value
    for (k, peer), (_, other) in zip(a_peers + [(0, None)], a_across):
        if k:
            send(mine, mine, g_send.at[0, k], g_recv.at[0, k], peer)
        send(mine, mine, g_send.at[1, k], g_recv.at[1, k], other)
    for k in range(n):
        if k:
            same = fin.at[piece(core, lax.rem(a_at + n - k, n))]
            pltpu.make_async_copy(same, same, g_recv.at[0, k]).wait()
        theirs = fin.at[piece(1 - core, lax.rem(b_at + n - k, n))]
        pltpu.make_async_copy(theirs, theirs, g_recv.at[1, k]).wait()

    for copy in copies:
        copy.wait_send()

    @pl.when(has_low)
    def _():
        for q in range(REACH):
            to_low(q).wait_send()

    @pl.when(has_high)
    def _():
        for q in range(REACH):
            to_high(q).wait_send()


def front(sizes, sketch, marginal_std, cov_tiles, tile_cols):
    rows, k = sketch.shape
    tile = cov_tiles.shape[1]
    ny, nx, nz = sizes["ny"], sizes["nx"], sizes["nzh"] * sizes["nzl"]
    total = rows * sizes["nx"] * ny * nz * 2
    count = 24
    chunk = count // ny
    vmem, dma = pltpu.VMEM, pltpu.SemaphoreType.DMA
    block = (LINES, tile, k)
    scratch = [
        pltpu.SMEM(tile_cols.shape, jnp.int32), vmem((LINES, 2, 128), F32), vmem(block, BF16), vmem(cov_tiles.shape, BF16), vmem((2 * REACH + LINES, tile, k), BF16),
        vmem((REACH, tile, k), BF16), vmem((REACH, tile, k), BF16),
        vmem((16, 128), F32), vmem((128, 16), F32), vmem(block, F32),
        vmem((k, 2 * k), F32),
        vmem((2 * count, 8, 128), F32),
        vmem((2, ny, chunk, 8, 128), F32), vmem((chunk, 8, 128), F32), vmem((nz, chunk, 8, 128), F32),
        vmem((chunk, 8, 128), F32), vmem((nx, chunk, 8, 128), F32),
        dma((4,)), dma((2 * REACH,)), dma((2 * REACH,)),
        dma((2, ny)), dma((2, ny)), dma((nz,)), dma((nz,)), dma((nx,)), dma((nx,)), dma((2, ny)), dma((2, ny)),
    ]
    in_hbm = pl.BlockSpec(memory_space=pltpu.HBM)
    in_vmem = pl.BlockSpec(memory_space=pltpu.VMEM)
    return pl.pallas_call(
        functools.partial(front_kernel, sizes, 1.0 / total),
        out_shape=(
            jax.ShapeDtypeStruct(block, BF16), jax.ShapeDtypeStruct(block, BF16),
            jax.ShapeDtypeStruct((2 * count, 8, 128), F32),
        ),
        in_specs=[in_hbm] * 4,
        out_specs=(in_vmem,) * 3,
        scratch_shapes=scratch,
        compiler_params=pltpu.CompilerParams(collective_id=0, has_side_effects=True, vmem_limit_bytes=48 * 2**20),
        name="front",
    )(*(pin_hbm(a) for a in (tile_cols, marginal_std.reshape(LINES, 2, 128), sketch.reshape(block), cov_tiles)))


def split3(a):
    a1 = a.astype(BF16)
    rest = a - a1.astype(F32)
    a2 = rest.astype(BF16)
    return a1, a2, (rest - a2.astype(F32)).astype(BF16)


def factor_in_place(work, rows_w, rows_f, n):
    def panel(p, carry):
        lane = lax.broadcasted_iota(jnp.int32, (8, 128), 1)
        sub = lax.broadcasted_iota(jnp.int32, (8, 128), 0)
        groups = PANEL // 8
        left = [work[0, 8 * g : 8 * g + 8] for g in range(groups)]
        right = [work[1, 8 * g : 8 * g + 8] for g in range(groups)]
        for m in range(PANEL // PIVOT):
            c0 = m * PIVOT
            g0, s0 = c0 // 8, c0 % 8
            inside = (lane >= c0) & (lane < c0 + PIVOT)
            row_l = [work[0, pl.ds(c0 + q, 8, stride=0), :] for q in range(PIVOT)]
            row_r = [work[1, pl.ds(c0 + q, 8, stride=0), :] for q in range(PIVOT)]

            def lane_of(v, at):
                return jnp.broadcast_to(v[:, at : at + 1], (8, 128))

            piv = {(r, q): lane_of(row_l[q], c0 + r) for q in range(PIVOT) for r in range(q, PIVOT)}
            cols = [[lane_of(left[g], c0 + q) for q in range(PIVOT)] for g in range(g0, groups)]
            row_l = [jnp.where(inside, jnp.where(lane == c0 + q, 1.0, 0.0), row_l[q]) for q in range(PIVOT)]
            u = {}
            inv = []
            for q in range(PIVOT):
                d = piv[q, q]
                i = lax.rsqrt(d)
                inv.append(i)
                u[q, q] = d * i
                for r in range(q + 1, PIVOT):
                    u[q, r] = piv[r, q] * i
                for r in range(q + 1, PIVOT):
                    for t in range(r, PIVOT):
                        piv[t, r] = piv[t, r] - u[q, r] * u[q, t]

            def sweep(v):
                out = []
                for q in range(PIVOT):
                    a = v[q]
                    for r in range(q):
                        a = a - u[r, q] * out[r]
                    out.append(a * inv[q])
                return out

            z_l, z_r = sweep(row_l), sweep(row_r)
            for q in range(PIVOT):
                row = pl.ds(c0 + q, 1)
                rows_w[p, row, 0:128] = z_l[q][0:1]
                rows_w[p, row, 128:n] = z_r[q][0:1]
                f = jnp.where(inside, 0.0, z_l[q])
                for r in range(q, PIVOT):
                    f = jnp.where(lane == c0 + r, u[q, r], f)
                rows_f[p, row, 0:128] = f[0:1]
                rows_f[p, row, 128:n] = z_r[q][0:1]
            for g in range(g0, groups):
                if g == g0 and s0 + PIVOT == 8:
                    continue
                w = sweep(cols[g - g0])
                if g == g0:
                    w = [jnp.where(sub >= s0 + PIVOT, v, 0.0) for v in w]
                cleared = jnp.where(inside & (sub >= s0 + PIVOT) if g == g0 else inside, 0.0, left[g])
                for q in range(PIVOT):
                    cleared = cleared - w[q] * z_l[q]
                    right[g] = right[g] - w[q] * z_r[q]
                left[g] = cleared
                if g == (c0 + PIVOT) // 8:
                    work[0, 8 * g : 8 * g + 8] = left[g]
                    work[1, 8 * g : 8 * g + 8] = right[g]

        at = lax.broadcasted_iota(jnp.int32, (PANEL, n), 1)
        below_diagonal = at <= lax.broadcasted_iota(jnp.int32, (PANEL, n), 0)
        b1, b2, b3 = split3(jnp.where(below_diagonal | (at >= PANEL), rows_w[p], 0.0))
        lhs = jnp.concatenate([b1, b1, b2, b2, b1, b3], axis=0)
        rhs = jnp.concatenate([b1, b2, b1, b2, b3, b1], axis=0)
        update = lax.dot_general(lhs, rhs, (((0,), (0,)), ((), ())), preferred_element_type=F32)
        lanes = lax.broadcasted_iota(jnp.int32, (n - PANEL, n), 1)
        old = jnp.concatenate([work[0, PANEL:], work[1, PANEL:]], axis=1)
        fresh = pltpu.roll(jnp.where(lanes < PANEL, 0.0, old) - update[PANEL:, :], n - PANEL, 1)
        work[0, 0 : n - PANEL] = fresh[:, 0:128]
        work[1, 0 : n - PANEL] = fresh[:, 128:]
        return carry

    lax.fori_loop(0, n // PANEL, panel, 0)


def back_kernel(cols_hbm, gram_ref, high_v, low_v, basis_hbm, factor_hbm,
                cols_ref, factor_ref, out_v, work, rows_w, rows_f, w_high, w_low, load_sem, out_sem):
    n = work.shape[1]
    half = n // 2
    load_cols = pltpu.make_async_copy(cols_hbm, cols_ref, load_sem.at[0])
    load_cols.start()
    upper = gram_ref[16:32].reshape(half, half)
    work[0, 0:half] = gram_ref[0:16].reshape(half, half)
    work[1, 0:half] = upper
    work[0, half:] = upper.T
    work[1, half:] = gram_ref[32:48].reshape(half, half)
    factor_in_place(work, rows_w, rows_f, n)

    for p in range(n // PANEL):
        rows = slice(p * PANEL, p * PANEL + PANEL)
        row = lax.broadcasted_iota(jnp.int32, (PANEL, n), 0) + p * PANEL
        col = lax.broadcasted_iota(jnp.int32, (PANEL, n), 1)
        w, f = rows_w[p], rows_f[p]
        if p:
            w, f = pltpu.roll(w, p * PANEL, 1), pltpu.roll(f, p * PANEL, 1)
        w = jnp.where(col <= row, w, 0.0)
        factor_ref[rows, :] = jnp.where(col >= row, f, 0.0)
        high = w.astype(BF16)
        w_high[rows, :] = high
        w_low[rows, :] = (w - high.astype(F32)).astype(BF16)

    load_cols.wait()
    writes = [pltpu.make_async_copy(factor_ref, factor_hbm, out_sem.at[LINES])]
    writes[0].start()
    wh, wl = w_high[...], w_low[...]
    weights = jnp.concatenate([wh, wl, wh], axis=1)
    for t in range(LINES):
        head = t // REACH * REACH
        start = cols_ref[head, REACH]
        start = start - start % REACH
        line = jnp.int32(head)
        for e in range(REACH):
            line += jnp.where(cols_ref[t, e] >= start, 1, 0)
        line = jnp.clip(line, 0, LINES - 1)
        h, l = high_v[line], low_v[line]
        out_v[t] = lax.dot_general(
            jnp.concatenate([h, h, l], axis=1), weights, (((1,), (1,)), ((), ())), preferred_element_type=F32
        )
        writes.append(pltpu.make_async_copy(out_v.at[t], basis_hbm.at[t], out_sem.at[t]))
        writes[-1].start()
    for copy in writes:
        copy.wait()


def back(tile_cols, gram, high, low):
    lines, tile, k = high.shape
    vmem, dma = pltpu.VMEM, pltpu.SemaphoreType.DMA
    in_hbm = pl.BlockSpec(memory_space=pltpu.HBM)
    in_vmem = pl.BlockSpec(memory_space=pltpu.VMEM)
    return pl.pallas_call(
        back_kernel,
        out_shape=(jax.ShapeDtypeStruct((lines, tile, k), F32), jax.ShapeDtypeStruct((k, k), F32)),
        in_specs=[in_hbm, in_vmem, in_vmem, in_vmem],
        out_specs=(in_hbm, in_hbm),
        scratch_shapes=[
            pltpu.SMEM(tile_cols.shape, jnp.int32), vmem((k, k), F32), vmem((lines, tile, k), F32),
            vmem((2, k, k // 2), F32), vmem((k // PANEL, PANEL, k), F32), vmem((k // PANEL, PANEL, k), F32),
            vmem((k, k), BF16), vmem((k, k), BF16), dma((1,)), dma((lines + 1,)),
        ],
        compiler_params=pltpu.CompilerParams(vmem_limit_bytes=48 * 2**20),
        name="back",
    )(pin_hbm(tile_cols), gram, high, low)


def per_device(sizes, sketch, marginal_std, cov_tiles, tile_cols):
    high, low, gram = front(sizes, sketch, marginal_std, cov_tiles, tile_cols)
    basis, factor = back(tile_cols, gram, high, low)
    return basis.reshape(sketch.shape), factor


def build(mesh, sizes):
    in_specs = (P(("grp", "dev"), None), P(("grp", "dev")), P(), P(("grp", "dev"), None))
    out_specs = (P(("grp", "dev"), None), P())
    return jax.shard_map(
        functools.partial(per_device, sizes), mesh=mesh, in_specs=in_specs, out_specs=out_specs, check_vma=False
    )


def solution(mesh):
    return build(mesh, SIZES)
```

```python
import functools

import jax
import jax.numpy as jnp
from jax import lax
from jax.experimental import pallas as pl
from jax.experimental.pallas import tpu as pltpu
from jax.sharding import PartitionSpec as P

MESH = pl.DeviceIdType.MESH
F32, BF16 = jnp.float32, jnp.bfloat16
REACH = 4
LINES = 8
LAGS = 9
PANEL = 32
PIVOT = 8

SIZES = dict(nx=4, ny=8, nzh=4, nzl=2)


def pin_hbm(a):
    return pltpu.with_memory_space_constraint(a, pltpu.HBM)


def far_first(n):
    return sorted(range(1, n), key=lambda k: -min(k, n - k))


def front_kernel(
    sizes, scale, cols_hbm, std_hbm, sketch_hbm, cov_hbm, high_v, low_v, fin,
    cols_ref, std_ref, sketch_v, cov_v, own, near, far, std_sorted, std_rows, acc, gacc,
    packed, got_a, sum_a, got_b, sum_b, got_x,
    load_sem, halo_send, halo_recv, send_sem, recv_sem,
):
    nx, ny, nzh, nzl = sizes["nx"], sizes["ny"], sizes["nzh"], sizes["nzl"]
    nz = nzh * nzl
    grp, dev = lax.axis_index("grp"), lax.axis_index("dev")
    per_grp = nx * nzh * 2
    total = per_grp * ny * nzl
    me = grp * per_grp + dev
    y, z_lo = lax.rem(grp, ny), lax.div(grp, ny)
    core = lax.rem(dev, 2)
    z_hi, x = lax.rem(lax.div(dev, 2), nzh), lax.div(dev, 2 * nzh)
    z = z_hi * nzl + z_lo

    def place(x_, y_, z_, core_):
        return (lax.rem(z_, nzl) * ny + y_, (x_ * nzh + lax.div(z_, nzl)) * 2 + core_)

    def linear(i):
        return (lax.div(i, per_grp), lax.rem(i, per_grp))

    outer = jnp.where(core == 0, me - 1, me + 1)
    has_outer = (outer >= 0) & (outer < total)

    load_cols = pltpu.make_async_copy(cols_hbm, cols_ref, load_sem.at[0])
    load_std = pltpu.make_async_copy(std_hbm, std_ref, load_sem.at[1])
    load_sketch = pltpu.make_async_copy(sketch_hbm, sketch_v, load_sem.at[2])
    load_cov = pltpu.make_async_copy(cov_hbm, cov_v, load_sem.at[3])
    for copy in (load_cols, load_std, load_sketch, load_cov):
        copy.start()

    barrier = pltpu.get_barrier_semaphore()

    def greet(device):
        pl.semaphore_signal(barrier, inc=1, device_id=device, device_id_type=MESH)

    y_peers = [(k, place(x, lax.rem(y + k, ny), z, core)) for k in far_first(ny)]
    z_peers = [(k, place(x, y, lax.rem(z + k, nz), core)) for k in far_first(nz)]
    x_peers = [(k, place(lax.rem(x + k, nx), y, z, core)) for k in far_first(nx)]
    y_across = [(k, place(x, lax.rem(y + k, ny), z, 1 - core)) for k in far_first(ny) + [0]]
    z_across = [(k, place(x, y, lax.rem(z + k, nz), 1 - core)) for k in far_first(nz) + [0]]
    for _, peer in z_peers + y_peers + x_peers + y_across + z_across[:-1]:
        greet(peer)

    @pl.when(has_outer)
    def _():
        greet(linear(outer))

    gacc[...] = jnp.zeros_like(gacc)
    zero_lines = jnp.zeros((REACH,) + own.shape[1:], BF16)
    own[0:REACH] = zero_lines
    own[REACH + LINES :] = zero_lines

    @pl.when(jnp.logical_not(has_outer))
    def _():
        far[...] = zero_lines

    load_cols.wait()
    tile_of_line = []
    for block in range(LINES // REACH):
        head = block * REACH
        start = cols_ref[head, REACH]
        offset = jnp.int32(0)
        for e in range(REACH):
            offset += jnp.where(cols_ref[head, e] >= start, 1, 0)
        for j in range(REACH):
            tile = cols_ref[head, REACH - offset + j] - start
            tile_of_line.append(jnp.clip(tile, 0, REACH - 1) + head)

    load_std.wait()
    for j in range(LINES):
        std_sorted[2 * j : 2 * j + 2, :] = std_ref[tile_of_line[j]]
    std_cols = std_sorted[...].T

    def times_std(value, j):
        return value * jnp.concatenate([std_rows[j], std_rows[j]], axis=1)

    def scale_lines(q):
        for j in (q, LINES - 1 - q):
            both = [jnp.broadcast_to(std_cols[:, c : c + 1], (128, 128)) for c in (2 * j, 2 * j + 1)]
            std_rows[j] = jnp.concatenate(both, axis=0)
            own[REACH + j] = times_std(sketch_v[tile_of_line[j]].astype(F32), j).astype(BF16)

    load_sketch.wait()
    scale_lines(0)
    scale_lines(1)

    n, a_at, b_at = ny, jnp.where(core == 0, y, z), jnp.where(core == 0, z, y)

    def cross(first, second):
        return [
            (k, tuple(jnp.where(core == 0, p, q) for p, q in zip(one, two)))
            for (k, one), (_, two) in zip(first, second)
        ]

    a_peers, b_peers = cross(y_peers, z_peers), cross(z_peers, y_peers)
    a_across, b_across = cross(y_across, z_across), cross(z_across, y_across)

    peers = len(z_peers + y_peers + x_peers + y_across + z_across) - 1
    pl.semaphore_wait(barrier, peers + jnp.where(has_outer, 1, 0))

    def to_near(q):
        return pltpu.make_async_remote_copy(
            src_ref=own.at[REACH + jnp.where(core == 0, LINES - 1 - q, q)], dst_ref=near.at[q], send_sem=halo_send.at[q],
            recv_sem=halo_recv.at[q], device_id=place(x, y, z, 1 - core), device_id_type=MESH,
        )

    def to_far(q):
        return pltpu.make_async_remote_copy(
            src_ref=own.at[REACH + jnp.where(core == 0, q, LINES - 1 - q)], dst_ref=far.at[q],
            send_sem=halo_send.at[REACH + q], recv_sem=halo_recv.at[REACH + q], device_id=linear(outer),
            device_id_type=MESH,
        )

    for q in range(REACH):
        @pl.when(has_outer)
        def _():
            to_far(q).start()

        to_near(q).start()
        if q + 2 < REACH:
            scale_lines(q + 2)

    load_cov.wait()

    def own_line(j, carry):
        lags = jnp.concatenate([cov_v[e] for e in range(LAGS)], axis=1)
        lines = own[pl.ds(j, LAGS)].reshape(LAGS * own.shape[1], own.shape[2])
        acc[j] = jnp.dot(lags, lines, preferred_element_type=F32)
        return carry

    lax.fori_loop(0, LINES, own_line, 0)

    def finish(j, product):
        latent = times_std(product, j)
        high = latent.astype(BF16)
        low = (latent - high.astype(F32)).astype(BF16)
        high_v[j] = high
        low_v[j] = low
        pair = jnp.concatenate([high, low], axis=1)
        gacc[...] += lax.dot_general(high, pair, (((0,), (0,)), ((), ())), preferred_element_type=F32)

    def add_line(line, q, upper):
        for t in range(REACH - q):
            j = jnp.where(upper, REACH + q + t, REACH - 1 - q - t)
            e = jnp.where(upper, LAGS - 1 - t, t)
            product = acc[j] + jnp.dot(cov_v[e], line, preferred_element_type=F32)
            if t:
                acc[j] = product
            else:
                finish(j, product)

    for q in range(REACH):
        to_near(q).wait_recv()
        add_line(near[q], q, core == 0)
    for q in range(REACH):
        @pl.when(has_outer)
        def _():
            to_far(q).wait_recv()

        add_line(far[q], q, core == 1)

    half = gacc.shape[0] // 2
    for block, (r, c) in enumerate(((0, 0), (0, half), (half, half))):
        hh = gacc[r : r + half, c : c + half]
        hl = gacc[r : r + half, 2 * half + c : 3 * half + c]
        lh = gacc[c : c + half, 2 * half + r : 3 * half + r].T
        packed[16 * block : 16 * block + 16] = ((hh + (hl + lh)) * scale).reshape(16, 8, 128)

    count = packed.shape[0] // 2
    chunk = count // n

    def send(source, target, step, peer):
        pltpu.make_async_remote_copy(
            src_ref=source, dst_ref=target, send_sem=send_sem.at[step], recv_sem=recv_sem.at[step], device_id=peer,
            device_id_type=MESH,
        ).start()

    def wait(sem, chunks):
        bytes_of = packed.at[pl.ds(0, chunks * chunk)]
        pltpu.make_async_copy(bytes_of, bytes_of, sem).wait()

    def piece(half_of, at):
        return pl.ds(half_of * count + at * chunk, chunk)

    for (k, peer), (_, other) in zip(a_peers + [(0, None)], b_across):
        if k:
            own_piece = packed.at[piece(core, lax.rem(a_at + k, n))]
            send(own_piece, got_a.at[0, k], 0, peer)
        their_piece = packed.at[piece(1 - core, lax.rem(b_at + k, n))]
        send(their_piece, got_a.at[1, k], 0, other)
    value = packed[piece(core, a_at)]
    wait(recv_sem.at[0], 2 * n - 1)
    for k in range(n):
        for side in (0, 1) if k else (1,):
            value = value + got_a[side, k]

    def gather_sum(value, here, peers_, source, slots, step):
        source[...] = value
        for _, peer in peers_:
            send(source, slots.at[here], step, peer)
        slots[pl.ds(here, 1)] = value[None]
        wait(recv_sem.at[step], slots.shape[0] - 1)
        out = slots[0]
        for i in range(1, slots.shape[0]):
            out = out + slots[i]
        return out

    value = gather_sum(value, b_at, b_peers, sum_a, got_b, 1)
    value = gather_sum(value, x, x_peers, sum_b, got_x, 2)

    mine = fin.at[piece(core, a_at)]
    fin[piece(core, a_at)] = value
    for (k, peer), (_, other) in zip(a_peers + [(0, None)], a_across):
        if k:
            send(mine, mine, 3, peer)
        send(mine, mine, 3, other)
    wait(recv_sem.at[3], 2 * n - 1)
    for step, chunks in enumerate((2 * n - 1, n - 1, nx - 1, 2 * n - 1)):
        wait(send_sem.at[step], chunks)

    for q in range(REACH):
        to_near(q).wait_send()

    @pl.when(has_outer)
    def _():
        for q in range(REACH):
            to_far(q).wait_send()


def front(sizes, sketch, marginal_std, cov_tiles, tile_cols):
    rows, k = sketch.shape
    tile = cov_tiles.shape[1]
    ny, nx, nz = sizes["ny"], sizes["nx"], sizes["nzh"] * sizes["nzl"]
    total = rows * sizes["nx"] * ny * nz * 2
    count = 24
    chunk = count // ny
    vmem, dma = pltpu.VMEM, pltpu.SemaphoreType.DMA
    block = (LINES, tile, k)
    scratch = [
        pltpu.SMEM(tile_cols.shape, jnp.int32), vmem((LINES, 2, 128), F32), vmem(block, BF16), vmem(cov_tiles.shape, BF16), vmem((2 * REACH + LINES, tile, k), BF16),
        vmem((REACH, tile, k), BF16), vmem((REACH, tile, k), BF16),
        vmem((16, 128), F32), vmem((LINES, tile, 128), F32), vmem(block, F32),
        vmem((k, 2 * k), F32),
        vmem((2 * count, 8, 128), F32),
        vmem((2, ny, chunk, 8, 128), F32), vmem((chunk, 8, 128), F32), vmem((nz, chunk, 8, 128), F32),
        vmem((chunk, 8, 128), F32), vmem((nx, chunk, 8, 128), F32),
        dma((4,)), dma((2 * REACH,)), dma((2 * REACH,)),
        dma((4,)), dma((4,)),
    ]
    in_hbm = pl.BlockSpec(memory_space=pltpu.HBM)
    in_vmem = pl.BlockSpec(memory_space=pltpu.VMEM)
    return pl.pallas_call(
        functools.partial(front_kernel, sizes, 1.0 / total),
        out_shape=(
            jax.ShapeDtypeStruct(block, BF16), jax.ShapeDtypeStruct(block, BF16),
            jax.ShapeDtypeStruct((2 * count, 8, 128), F32),
        ),
        in_specs=[in_hbm] * 4,
        out_specs=(in_vmem,) * 3,
        scratch_shapes=scratch,
        compiler_params=pltpu.CompilerParams(collective_id=0, has_side_effects=True, vmem_limit_bytes=48 * 2**20),
        name="front",
    )(*(pin_hbm(a) for a in (tile_cols, marginal_std.reshape(LINES, 2, 128), sketch.reshape(block), cov_tiles)))


def split3(a):
    a1 = a.astype(BF16)
    rest = a - a1.astype(F32)
    a2 = rest.astype(BF16)
    return a1, a2, (rest - a2.astype(F32)).astype(BF16)


def stacked(b):
    b1, b2, b3 = split3(b)
    return jnp.concatenate([b1, b1, b2, b2, b1, b3], axis=0), jnp.concatenate([b1, b2, b1, b2, b3, b1], axis=0)


def factor_in_place(work, rest, late, rows_w, rows_f, n):
    def panel(p, carry):
        lanes = lax.broadcasted_iota(jnp.int32, (n - PANEL, n), 1)
        lhs, rhs = stacked(late[...])
        update = lax.dot_general(lhs, rhs, (((0,), (0,)), ((), ())), preferred_element_type=F32)
        old = jnp.concatenate([rest[0], rest[1]], axis=1)
        fresh = jnp.where(lanes >= jnp.where(p > 0, n - PANEL, n), 0.0, old) - update[PANEL:]
        following = pltpu.roll(jnp.where(lanes[:PANEL] < PANEL, 0.0, fresh[:PANEL]), n - PANEL, 1)
        fresh = pltpu.roll(fresh[PANEL:], n - PANEL, 1)
        rest[0, 0 : n - 2 * PANEL] = fresh[:, 0:128]
        rest[1, 0 : n - 2 * PANEL] = fresh[:, 128:]

        lane = lax.broadcasted_iota(jnp.int32, (8, 128), 1)
        sub = lax.broadcasted_iota(jnp.int32, (8, 128), 0)
        groups = PANEL // 8
        left = [work[0, 8 * g : 8 * g + 8] for g in range(groups)]
        right = [work[1, 8 * g : 8 * g + 8] for g in range(groups)]
        for m in range(PANEL // PIVOT):
            c0 = m * PIVOT
            g0, s0 = c0 // 8, c0 % 8
            inside = (lane >= c0) & (lane < c0 + PIVOT)
            row_l = [work[0, pl.ds(c0 + q, 8, stride=0), :] for q in range(PIVOT)]
            row_r = [work[1, pl.ds(c0 + q, 8, stride=0), :] for q in range(PIVOT)]

            def lane_of(v, at):
                return jnp.broadcast_to(v[:, at : at + 1], (8, 128))

            piv = {(r, q): lane_of(row_l[q], c0 + r) for q in range(PIVOT) for r in range(q, PIVOT)}
            cols = [[lane_of(left[g], c0 + q) for q in range(PIVOT)] for g in range(g0, groups)]
            row_l = [jnp.where(inside, jnp.where(lane == c0 + q, 1.0, 0.0), row_l[q]) for q in range(PIVOT)]
            u = {}
            inv = []
            for q in range(PIVOT):
                d = piv[q, q]
                i = lax.rsqrt(d)
                inv.append(i)
                u[q, q] = d * i
                for r in range(q + 1, PIVOT):
                    u[q, r] = piv[r, q] * i
                for r in range(q + 1, PIVOT):
                    for t in range(r, PIVOT):
                        piv[t, r] = piv[t, r] - u[q, r] * u[q, t]

            def sweep(v):
                out = []
                for q in range(PIVOT):
                    a = v[q]
                    for r in range(q):
                        a = a - u[r, q] * out[r]
                    out.append(a * inv[q])
                return out

            z_l, z_r = sweep(row_l), sweep(row_r)
            for q in range(PIVOT):
                row = pl.ds(c0 + q, 1)
                rows_w[p, row, 0:128] = z_l[q][0:1]
                rows_w[p, row, 128:n] = z_r[q][0:1]
                f = jnp.where(inside, 0.0, z_l[q])
                for r in range(q, PIVOT):
                    f = jnp.where(lane == c0 + r, u[q, r], f)
                rows_f[p, row, 0:128] = f[0:1]
                rows_f[p, row, 128:n] = z_r[q][0:1]
            for g in range(g0, groups):
                if g == g0 and s0 + PIVOT == 8:
                    continue
                w = sweep(cols[g - g0])
                if g == g0:
                    w = [jnp.where(sub >= s0 + PIVOT, v, 0.0) for v in w]
                cleared = jnp.where(inside & (sub >= s0 + PIVOT) if g == g0 else inside, 0.0, left[g])
                for q in range(PIVOT):
                    cleared = cleared - w[q] * z_l[q]
                    right[g] = right[g] - w[q] * z_r[q]
                left[g] = cleared
                if g == (c0 + PIVOT) // 8:
                    work[0, 8 * g : 8 * g + 8] = left[g]
                    work[1, 8 * g : 8 * g + 8] = right[g]

        at = lax.broadcasted_iota(jnp.int32, (PANEL, n), 1)
        below_diagonal = at <= lax.broadcasted_iota(jnp.int32, (PANEL, n), 0)
        rows = jnp.where(below_diagonal | (at >= PANEL), rows_w[p], 0.0)
        lhs, rhs = stacked(rows)
        update = lax.dot_general(lhs[:, 0:128], rhs, (((0,), (0,)), ((), ())), preferred_element_type=F32)
        following = following - pltpu.roll(update[PANEL : 2 * PANEL], n - PANEL, 1)
        work[0] = following[:, 0:128]
        work[1] = following[:, 128:]
        late[...] = pltpu.roll(rows, n - PANEL, 1)
        return carry

    late[...] = jnp.zeros_like(late)
    lax.fori_loop(0, n // PANEL, panel, 0)


def back_kernel(cols_hbm, gram_ref, high_v, low_v, basis_hbm, factor_hbm,
                cols_ref, factor_ref, out_v, work, rest, late, rows_w, rows_f, w_high, w_low, load_sem, out_sem):
    n = factor_ref.shape[0]
    half = n // 2
    load_cols = pltpu.make_async_copy(cols_hbm, cols_ref, load_sem.at[0])
    load_cols.start()
    upper = gram_ref[16:32].reshape(half, half)
    first = gram_ref[0:16].reshape(half, half)
    work[0] = first[:PANEL]
    work[1] = upper[:PANEL]
    rest[0, 0 : half - PANEL] = first[PANEL:]
    rest[1, 0 : half - PANEL] = upper[PANEL:]
    rest[0, half - PANEL :] = upper.T
    rest[1, half - PANEL :] = gram_ref[32:48].reshape(half, half)
    factor_in_place(work, rest, late, rows_w, rows_f, n)

    for p in range(n // PANEL):
        rows = slice(p * PANEL, p * PANEL + PANEL)
        row = lax.broadcasted_iota(jnp.int32, (PANEL, n), 0) + p * PANEL
        col = lax.broadcasted_iota(jnp.int32, (PANEL, n), 1)
        w, f = rows_w[p], rows_f[p]
        if p:
            w, f = pltpu.roll(w, p * PANEL, 1), pltpu.roll(f, p * PANEL, 1)
        w = jnp.where(col <= row, w, 0.0)
        factor_ref[rows, :] = jnp.where(col >= row, f, 0.0)
        high = w.astype(BF16)
        w_high[rows, :] = high
        w_low[rows, :] = (w - high.astype(F32)).astype(BF16)

    load_cols.wait()
    writes = [pltpu.make_async_copy(factor_ref, factor_hbm, out_sem.at[LINES])]
    writes[0].start()
    wh, wl = w_high[...], w_low[...]
    weights = jnp.concatenate([wh, wl, wh], axis=1)
    for t in range(LINES):
        head = t // REACH * REACH
        start = cols_ref[head, REACH]
        start = start - start % REACH
        line = jnp.int32(head)
        for e in range(REACH):
            line += jnp.where(cols_ref[t, e] >= start, 1, 0)
        line = jnp.clip(line, 0, LINES - 1)
        h, l = high_v[line], low_v[line]
        out_v[t] = lax.dot_general(
            jnp.concatenate([h, h, l], axis=1), weights, (((1,), (1,)), ((), ())), preferred_element_type=F32
        )
        writes.append(pltpu.make_async_copy(out_v.at[t], basis_hbm.at[t], out_sem.at[t]))
        writes[-1].start()
    for copy in writes:
        copy.wait()


def back(tile_cols, gram, high, low):
    lines, tile, k = high.shape
    vmem, dma = pltpu.VMEM, pltpu.SemaphoreType.DMA
    in_hbm = pl.BlockSpec(memory_space=pltpu.HBM)
    in_vmem = pl.BlockSpec(memory_space=pltpu.VMEM)
    return pl.pallas_call(
        back_kernel,
        out_shape=(jax.ShapeDtypeStruct((lines, tile, k), F32), jax.ShapeDtypeStruct((k, k), F32)),
        in_specs=[in_hbm, in_vmem, in_vmem, in_vmem],
        out_specs=(in_hbm, in_hbm),
        scratch_shapes=[
            pltpu.SMEM(tile_cols.shape, jnp.int32), vmem((k, k), F32), vmem((lines, tile, k), F32),
            vmem((2, PANEL, k // 2), F32), vmem((2, k - PANEL, k // 2), F32), vmem((PANEL, k), F32),
            vmem((k // PANEL, PANEL, k), F32), vmem((k // PANEL, PANEL, k), F32),
            vmem((k, k), BF16), vmem((k, k), BF16), dma((1,)), dma((lines + 1,)),
        ],
        compiler_params=pltpu.CompilerParams(vmem_limit_bytes=48 * 2**20),
        name="back",
    )(pin_hbm(tile_cols), gram, high, low)


def per_device(sizes, sketch, marginal_std, cov_tiles, tile_cols):
    high, low, gram = front(sizes, sketch, marginal_std, cov_tiles, tile_cols)
    basis, factor = back(tile_cols, gram, high, low)
    return basis.reshape(sketch.shape), factor


def build(mesh, sizes):
    in_specs = (P(("grp", "dev"), None), P(("grp", "dev")), P(), P(("grp", "dev"), None))
    out_specs = (P(("grp", "dev"), None), P())
    return jax.shard_map(
        functools.partial(per_device, sizes), mesh=mesh, in_specs=in_specs, out_specs=out_specs, check_vma=False
    )


def solution(mesh):
    return build(mesh, SIZES)
```

```python
import functools

import jax
import jax.numpy as jnp
from jax import lax
from jax.experimental import pallas as pl
from jax.experimental.pallas import tpu as pltpu
from jax.sharding import PartitionSpec as P

MESH = pl.DeviceIdType.MESH
F32, BF16 = jnp.float32, jnp.bfloat16
REACH = 4
LINES = 8
LAGS = 9
PANEL = 32
PIVOT = 8

SIZES = dict(nx=4, ny=8, nzh=4, nzl=2)


def pin_hbm(a):
    return pltpu.with_memory_space_constraint(a, pltpu.HBM)


def far_first(n):
    return sorted(range(1, n), key=lambda k: -min(k, n - k))


def front_kernel(
    sizes, scale, cols_hbm, std_hbm, sketch_hbm, cov_hbm, high_v, low_v, fin,
    cols_ref, std_ref, sketch_v, cov_v, own, near, far, std_sorted, std_rows, acc, gacc,
    packed, got_a, sum_a, got_b, sum_b, got_x,
    load_sem, halo_send, halo_recv, send_sem, recv_sem,
):
    nx, ny, nzh, nzl = sizes["nx"], sizes["ny"], sizes["nzh"], sizes["nzl"]
    nz = nzh * nzl
    grp, dev = lax.axis_index("grp"), lax.axis_index("dev")
    per_grp = nx * nzh * 2
    total = per_grp * ny * nzl
    me = grp * per_grp + dev
    y, z_lo = lax.rem(grp, ny), lax.div(grp, ny)
    core = lax.rem(dev, 2)
    z_hi, x = lax.rem(lax.div(dev, 2), nzh), lax.div(dev, 2 * nzh)
    z = z_hi * nzl + z_lo

    def place(x_, y_, z_, core_):
        return (lax.rem(z_, nzl) * ny + y_, (x_ * nzh + lax.div(z_, nzl)) * 2 + core_)

    def linear(i):
        return (lax.div(i, per_grp), lax.rem(i, per_grp))

    outer = jnp.where(core == 0, me - 1, me + 1)
    has_outer = (outer >= 0) & (outer < total)

    load_cols = pltpu.make_async_copy(cols_hbm, cols_ref, load_sem.at[0])
    load_std = pltpu.make_async_copy(std_hbm, std_ref, load_sem.at[1])
    load_sketch = pltpu.make_async_copy(sketch_hbm, sketch_v, load_sem.at[2])
    load_cov = pltpu.make_async_copy(cov_hbm, cov_v, load_sem.at[3])
    for copy in (load_cols, load_std, load_sketch):
        copy.start()

    barrier = pltpu.get_barrier_semaphore()

    def greet(device):
        pl.semaphore_signal(barrier, inc=1, device_id=device, device_id_type=MESH)

    y_peers = [(k, place(x, lax.rem(y + k, ny), z, core)) for k in far_first(ny)]
    z_peers = [(k, place(x, y, lax.rem(z + k, nz), core)) for k in far_first(nz)]
    x_peers = [(k, place(lax.rem(x + k, nx), y, z, core)) for k in far_first(nx)]
    y_across = [(k, place(x, lax.rem(y + k, ny), z, 1 - core)) for k in far_first(ny) + [0]]
    z_across = [(k, place(x, y, lax.rem(z + k, nz), 1 - core)) for k in far_first(nz) + [0]]
    for _, peer in z_peers + y_peers + x_peers + y_across + z_across[:-1]:
        greet(peer)

    @pl.when(has_outer)
    def _():
        greet(linear(outer))

    gacc[...] = jnp.zeros_like(gacc)
    zero_lines = jnp.zeros((REACH,) + own.shape[1:], BF16)
    own[0:REACH] = zero_lines
    own[REACH + LINES :] = zero_lines

    @pl.when(jnp.logical_not(has_outer))
    def _():
        far[...] = zero_lines

    load_cols.wait()
    tile_of_line = []
    for block in range(LINES // REACH):
        head = block * REACH
        start = cols_ref[head, REACH]
        offset = jnp.int32(0)
        for e in range(REACH):
            offset += jnp.where(cols_ref[head, e] >= start, 1, 0)
        for j in range(REACH):
            tile = cols_ref[head, REACH - offset + j] - start
            tile_of_line.append(jnp.clip(tile, 0, REACH - 1) + head)

    load_std.wait()
    for j in range(LINES):
        std_sorted[2 * j : 2 * j + 2, :] = std_ref[tile_of_line[j]]
    std_cols = std_sorted[...].T

    def times_std(value, j):
        return value * jnp.concatenate([std_rows[j], std_rows[j]], axis=1)

    def scale_lines(q):
        for j in (q, LINES - 1 - q):
            both = [jnp.broadcast_to(std_cols[:, c : c + 1], (128, 128)) for c in (2 * j, 2 * j + 1)]
            std_rows[j] = jnp.concatenate(both, axis=0)
            own[REACH + j] = times_std(sketch_v[tile_of_line[j]].astype(F32), j).astype(BF16)

    load_sketch.wait()
    load_cov.start()
    scale_lines(0)
    scale_lines(1)

    n, a_at, b_at = ny, jnp.where(core == 0, y, z), jnp.where(core == 0, z, y)

    def cross(first, second):
        return [
            (k, tuple(jnp.where(core == 0, p, q) for p, q in zip(one, two)))
            for (k, one), (_, two) in zip(first, second)
        ]

    a_peers, b_peers = cross(y_peers, z_peers), cross(z_peers, y_peers)
    a_across, b_across = cross(y_across, z_across), cross(z_across, y_across)

    peers = len(z_peers + y_peers + x_peers + y_across + z_across) - 1
    pl.semaphore_wait(barrier, peers + jnp.where(has_outer, 1, 0))

    def to_near(q):
        return pltpu.make_async_remote_copy(
            src_ref=own.at[REACH + jnp.where(core == 0, LINES - 1 - q, q)], dst_ref=near.at[q], send_sem=halo_send.at[0],
            recv_sem=halo_recv.at[q], device_id=place(x, y, z, 1 - core), device_id_type=MESH,
        )

    def to_far(q):
        return pltpu.make_async_remote_copy(
            src_ref=own.at[REACH + jnp.where(core == 0, q, LINES - 1 - q)], dst_ref=far.at[q],
            send_sem=halo_send.at[1], recv_sem=halo_recv.at[REACH + q], device_id=linear(outer),
            device_id_type=MESH,
        )

    for q in range(REACH):
        @pl.when(has_outer)
        def _():
            to_far(q).start()

        to_near(q).start()
        if q + 2 < REACH:
            scale_lines(q + 2)

    load_cov.wait()

    def own_line(j, carry):
        lags = jnp.concatenate([cov_v[e] for e in range(LAGS)], axis=1)
        lines = own[pl.ds(j, LAGS)].reshape(LAGS * own.shape[1], own.shape[2])
        acc[j] = jnp.dot(lags, lines, preferred_element_type=F32)
        return carry

    lax.fori_loop(0, LINES, own_line, 0)

    def finish(j, product):
        latent = times_std(product, j)
        high = latent.astype(BF16)
        low = (latent - high.astype(F32)).astype(BF16)
        high_v[j] = high
        low_v[j] = low
        pair = jnp.concatenate([high, low], axis=1)
        gacc[...] += lax.dot_general(high, pair, (((0,), (0,)), ((), ())), preferred_element_type=F32)

    def add_line(line, q, upper):
        for t in range(REACH - q):
            j = jnp.where(upper, REACH + q + t, REACH - 1 - q - t)
            e = jnp.where(upper, LAGS - 1 - t, t)
            product = acc[j] + jnp.dot(cov_v[e], line, preferred_element_type=F32)
            if t:
                acc[j] = product
            else:
                finish(j, product)

    for q in range(REACH):
        to_near(q).wait_recv()
        add_line(near[q], q, core == 0)
    for q in range(REACH):
        @pl.when(has_outer)
        def _():
            to_far(q).wait_recv()

        add_line(far[q], q, core == 1)

    half = gacc.shape[0] // 2
    for block, (r, c) in enumerate(((0, 0), (0, half), (half, half))):
        hh = gacc[r : r + half, c : c + half]
        hl = gacc[r : r + half, 2 * half + c : 3 * half + c]
        lh = gacc[c : c + half, 2 * half + r : 3 * half + r].T
        packed[16 * block : 16 * block + 16] = ((hh + (hl + lh)) * scale).reshape(16, 8, 128)

    count = packed.shape[0] // 2
    chunk = count // n

    def send(source, target, step, peer):
        pltpu.make_async_remote_copy(
            src_ref=source, dst_ref=target, send_sem=send_sem.at[step], recv_sem=recv_sem.at[step], device_id=peer,
            device_id_type=MESH,
        ).start()

    def wait(sem, chunks):
        bytes_of = packed.at[pl.ds(0, chunks * chunk)]
        pltpu.make_async_copy(bytes_of, bytes_of, sem).wait()

    def piece(half_of, at):
        return pl.ds(half_of * count + at * chunk, chunk)

    for (k, peer), (_, other) in zip(a_peers + [(0, None)], b_across):
        if k:
            own_piece = packed.at[piece(core, lax.rem(a_at + k, n))]
            send(own_piece, got_a.at[0, k], 0, peer)
        their_piece = packed.at[piece(1 - core, lax.rem(b_at + k, n))]
        send(their_piece, got_a.at[1, k], 0, other)
    value = packed[piece(core, a_at)]
    wait(recv_sem.at[0], 2 * n - 1)
    for k in range(n):
        for side in (0, 1) if k else (1,):
            value = value + got_a[side, k]

    def gather_sum(value, here, peers_, source, slots, step):
        source[...] = value
        for _, peer in peers_:
            send(source, slots.at[here], step, peer)
        slots[pl.ds(here, 1)] = value[None]
        wait(recv_sem.at[step], slots.shape[0] - 1)
        out = slots[0]
        for i in range(1, slots.shape[0]):
            out = out + slots[i]
        return out

    value = gather_sum(value, b_at, b_peers, sum_a, got_b, 1)
    value = gather_sum(value, x, x_peers, sum_b, got_x, 2)

    mine = fin.at[piece(core, a_at)]
    fin[piece(core, a_at)] = value
    for (k, peer), (_, other) in zip(a_peers + [(0, None)], a_across):
        if k:
            send(mine, mine, 3, peer)
        send(mine, mine, 3, other)
    wait(recv_sem.at[3], 2 * n - 1)
    for step, chunks in enumerate((2 * n - 1, n - 1, nx - 1, 2 * n - 1)):
        wait(send_sem.at[step], chunks)

    pltpu.make_async_copy(near, near, halo_send.at[0]).wait()

    @pl.when(has_outer)
    def _():
        pltpu.make_async_copy(far, far, halo_send.at[1]).wait()


def front(sizes, sketch, marginal_std, cov_tiles, tile_cols):
    rows, k = sketch.shape
    tile = cov_tiles.shape[1]
    ny, nx, nz = sizes["ny"], sizes["nx"], sizes["nzh"] * sizes["nzl"]
    total = rows * sizes["nx"] * ny * nz * 2
    count = 24
    chunk = count // ny
    vmem, dma = pltpu.VMEM, pltpu.SemaphoreType.DMA
    block = (LINES, tile, k)
    scratch = [
        pltpu.SMEM(tile_cols.shape, jnp.int32), vmem((LINES, 2, 128), F32), vmem(block, BF16), vmem(cov_tiles.shape, BF16), vmem((2 * REACH + LINES, tile, k), BF16),
        vmem((REACH, tile, k), BF16), vmem((REACH, tile, k), BF16),
        vmem((16, 128), F32), vmem((LINES, tile, 128), F32), vmem(block, F32),
        vmem((k, 2 * k), F32),
        vmem((2 * count, 8, 128), F32),
        vmem((2, ny, chunk, 8, 128), F32), vmem((chunk, 8, 128), F32), vmem((nz, chunk, 8, 128), F32),
        vmem((chunk, 8, 128), F32), vmem((nx, chunk, 8, 128), F32),
        dma((4,)), dma((2,)), dma((2 * REACH,)),
        dma((4,)), dma((4,)),
    ]
    in_hbm = pl.BlockSpec(memory_space=pltpu.HBM)
    in_vmem = pl.BlockSpec(memory_space=pltpu.VMEM)
    return pl.pallas_call(
        functools.partial(front_kernel, sizes, 1.0 / total),
        out_shape=(
            jax.ShapeDtypeStruct(block, BF16), jax.ShapeDtypeStruct(block, BF16),
            jax.ShapeDtypeStruct((2 * count, 8, 128), F32),
        ),
        in_specs=[in_hbm] * 4,
        out_specs=(in_vmem,) * 3,
        scratch_shapes=scratch,
        compiler_params=pltpu.CompilerParams(collective_id=0, has_side_effects=True, vmem_limit_bytes=48 * 2**20),
        name="front",
    )(*(pin_hbm(a) for a in (tile_cols, marginal_std.reshape(LINES, 2, 128), sketch.reshape(block), cov_tiles)))


def split3(a):
    a1 = a.astype(BF16)
    rest = a - a1.astype(F32)
    a2 = rest.astype(BF16)
    return a1, a2, (rest - a2.astype(F32)).astype(BF16)


def stacked(b):
    b1, b2, b3 = split3(b)
    return jnp.concatenate([b1, b1, b2, b2, b1, b3], axis=0), jnp.concatenate([b1, b2, b1, b2, b3, b1], axis=0)


def factor_in_place(work, rest, late, rows_w, rows_f, n):
    def panel(p, carry):
        lanes = lax.broadcasted_iota(jnp.int32, (n - PANEL, n), 1)
        lhs, rhs = stacked(late[...])
        update = lax.dot_general(lhs, rhs, (((0,), (0,)), ((), ())), preferred_element_type=F32)
        old = jnp.concatenate([rest[0], rest[1]], axis=1)
        fresh = jnp.where(lanes >= jnp.where(p > 0, n - PANEL, n), 0.0, old) - update[PANEL:]
        following = pltpu.roll(jnp.where(lanes[:PANEL] < PANEL, 0.0, fresh[:PANEL]), n - PANEL, 1)
        fresh = pltpu.roll(fresh[PANEL:], n - PANEL, 1)
        rest[0, 0 : n - 2 * PANEL] = fresh[:, 0:128]
        rest[1, 0 : n - 2 * PANEL] = fresh[:, 128:]

        lane = lax.broadcasted_iota(jnp.int32, (8, 128), 1)
        sub = lax.broadcasted_iota(jnp.int32, (8, 128), 0)
        groups = PANEL // 8
        left = [work[0, 8 * g : 8 * g + 8] for g in range(groups)]
        right = [work[1, 8 * g : 8 * g + 8] for g in range(groups)]
        for m in range(PANEL // PIVOT):
            c0 = m * PIVOT
            g0, s0 = c0 // 8, c0 % 8
            inside = (lane >= c0) & (lane < c0 + PIVOT)
            row_l = [work[0, pl.ds(c0 + q, 8, stride=0), :] for q in range(PIVOT)]
            row_r = [work[1, pl.ds(c0 + q, 8, stride=0), :] for q in range(PIVOT)]

            def lane_of(v, at):
                return jnp.broadcast_to(v[:, at : at + 1], (8, 128))

            piv = {(r, q): lane_of(row_l[q], c0 + r) for q in range(PIVOT) for r in range(q, PIVOT)}
            cols = [[lane_of(left[g], c0 + q) for q in range(PIVOT)] for g in range(g0, groups)]
            row_l = [jnp.where(inside, jnp.where(lane == c0 + q, 1.0, 0.0), row_l[q]) for q in range(PIVOT)]
            u = {}
            inv = []
            for q in range(PIVOT):
                d = piv[q, q]
                i = lax.rsqrt(d)
                inv.append(i)
                u[q, q] = d * i
                for r in range(q + 1, PIVOT):
                    u[q, r] = piv[r, q] * i
                for r in range(q + 1, PIVOT):
                    for t in range(r, PIVOT):
                        piv[t, r] = piv[t, r] - u[q, r] * u[q, t]

            def sweep(v):
                out = []
                for q in range(PIVOT):
                    a = v[q]
                    for r in range(q):
                        a = a - u[r, q] * out[r]
                    out.append(a * inv[q])
                return out

            z_l, z_r = sweep(row_l), sweep(row_r)
            for q in range(PIVOT):
                row = pl.ds(c0 + q, 1)
                rows_w[p, row, 0:128] = z_l[q][0:1]
                rows_w[p, row, 128:n] = z_r[q][0:1]
                f = jnp.where(inside, 0.0, z_l[q])
                for r in range(q, PIVOT):
                    f = jnp.where(lane == c0 + r, u[q, r], f)
                rows_f[p, row, 0:128] = f[0:1]
                rows_f[p, row, 128:n] = z_r[q][0:1]
            for g in range(g0, groups):
                if g == g0 and s0 + PIVOT == 8:
                    continue
                w = sweep(cols[g - g0])
                if g == g0:
                    w = [jnp.where(sub >= s0 + PIVOT, v, 0.0) for v in w]
                cleared = jnp.where(inside & (sub >= s0 + PIVOT) if g == g0 else inside, 0.0, left[g])
                for q in range(PIVOT):
                    cleared = cleared - w[q] * z_l[q]
                    right[g] = right[g] - w[q] * z_r[q]
                left[g] = cleared
                if g == (c0 + PIVOT) // 8:
                    work[0, 8 * g : 8 * g + 8] = left[g]
                    work[1, 8 * g : 8 * g + 8] = right[g]

        at = lax.broadcasted_iota(jnp.int32, (PANEL, n), 1)
        below_diagonal = at <= lax.broadcasted_iota(jnp.int32, (PANEL, n), 0)
        rows = jnp.where(below_diagonal | (at >= PANEL), rows_w[p], 0.0)
        lhs, rhs = stacked(rows)
        update = lax.dot_general(lhs[:, 0:128], rhs, (((0,), (0,)), ((), ())), preferred_element_type=F32)
        following = following - pltpu.roll(update[PANEL : 2 * PANEL], n - PANEL, 1)
        work[0] = following[:, 0:128]
        work[1] = following[:, 128:]
        late[...] = pltpu.roll(rows, n - PANEL, 1)
        return carry

    late[...] = jnp.zeros_like(late)
    lax.fori_loop(0, n // PANEL, panel, 0)


def back_kernel(cols_hbm, gram_ref, high_v, low_v, basis_hbm, factor_hbm,
                cols_ref, factor_ref, out_v, work, rest, late, rows_w, rows_f, w_high, w_low, load_sem, out_sem):
    n = factor_ref.shape[0]
    half = n // 2
    load_cols = pltpu.make_async_copy(cols_hbm, cols_ref, load_sem.at[0])
    load_cols.start()
    upper = gram_ref[16:32].reshape(half, half)
    first = gram_ref[0:16].reshape(half, half)
    work[0] = first[:PANEL]
    work[1] = upper[:PANEL]
    rest[0, 0 : half - PANEL] = first[PANEL:]
    rest[1, 0 : half - PANEL] = upper[PANEL:]
    rest[0, half - PANEL :] = upper.T
    rest[1, half - PANEL :] = gram_ref[32:48].reshape(half, half)
    factor_in_place(work, rest, late, rows_w, rows_f, n)

    for p in range(n // PANEL):
        rows = slice(p * PANEL, p * PANEL + PANEL)
        row = lax.broadcasted_iota(jnp.int32, (PANEL, n), 0) + p * PANEL
        col = lax.broadcasted_iota(jnp.int32, (PANEL, n), 1)
        w, f = rows_w[p], rows_f[p]
        if p:
            w, f = pltpu.roll(w, p * PANEL, 1), pltpu.roll(f, p * PANEL, 1)
        w = jnp.where(col <= row, w, 0.0)
        factor_ref[rows, :] = jnp.where(col >= row, f, 0.0)
        high = w.astype(BF16)
        w_high[rows, :] = high
        w_low[rows, :] = (w - high.astype(F32)).astype(BF16)

    load_cols.wait()
    writes = [pltpu.make_async_copy(factor_ref, factor_hbm, out_sem.at[LINES])]
    writes[0].start()
    wh, wl = w_high[...], w_low[...]
    weights = jnp.concatenate([wh, wl, wh], axis=1)
    for t in range(LINES):
        head = t // REACH * REACH
        start = cols_ref[head, REACH]
        start = start - start % REACH
        line = jnp.int32(head)
        for e in range(REACH):
            line += jnp.where(cols_ref[t, e] >= start, 1, 0)
        line = jnp.clip(line, 0, LINES - 1)
        h, l = high_v[line], low_v[line]
        out_v[t] = lax.dot_general(
            jnp.concatenate([h, h, l], axis=1), weights, (((1,), (1,)), ((), ())), preferred_element_type=F32
        )
        writes.append(pltpu.make_async_copy(out_v.at[t], basis_hbm.at[t], out_sem.at[t]))
        writes[-1].start()
    for copy in writes:
        copy.wait()


def back(tile_cols, gram, high, low):
    lines, tile, k = high.shape
    vmem, dma = pltpu.VMEM, pltpu.SemaphoreType.DMA
    in_hbm = pl.BlockSpec(memory_space=pltpu.HBM)
    in_vmem = pl.BlockSpec(memory_space=pltpu.VMEM)
    return pl.pallas_call(
        back_kernel,
        out_shape=(jax.ShapeDtypeStruct((lines, tile, k), F32), jax.ShapeDtypeStruct((k, k), F32)),
        in_specs=[in_hbm, in_vmem, in_vmem, in_vmem],
        out_specs=(in_hbm, in_hbm),
        scratch_shapes=[
            pltpu.SMEM(tile_cols.shape, jnp.int32), vmem((k, k), F32), vmem((lines, tile, k), F32),
            vmem((2, PANEL, k // 2), F32), vmem((2, k - PANEL, k // 2), F32), vmem((PANEL, k), F32),
            vmem((k // PANEL, PANEL, k), F32), vmem((k // PANEL, PANEL, k), F32),
            vmem((k, k), BF16), vmem((k, k), BF16), dma((1,)), dma((lines + 1,)),
        ],
        compiler_params=pltpu.CompilerParams(vmem_limit_bytes=48 * 2**20),
        name="back",
    )(pin_hbm(tile_cols), gram, high, low)


def per_device(sizes, sketch, marginal_std, cov_tiles, tile_cols):
    high, low, gram = front(sizes, sketch, marginal_std, cov_tiles, tile_cols)
    basis, factor = back(tile_cols, gram, high, low)
    return basis.reshape(sketch.shape), factor


def build(mesh, sizes):
    in_specs = (P(("grp", "dev"), None), P(("grp", "dev")), P(), P(("grp", "dev"), None))
    out_specs = (P(("grp", "dev"), None), P())
    return jax.shard_map(
        functools.partial(per_device, sizes), mesh=mesh, in_specs=in_specs, out_specs=out_specs, check_vma=False
    )


def solution(mesh):
    return build(mesh, SIZES)
```
